128 devices in a mesh: dp: 8 (over z_hi, y), fsdp: 16 (over x, z_lo, core).
Axes of the slice: x: 4, y: 4, z: 4 (z_hi: 2, z_lo: 2; z = z_hi * 2 + z_lo), core: 2. Of those that a mesh axis runs over, the one named last changes fastest.
Arguments:
- tokens: bfloat16 [65536, 8192], P(('dp', 'fsdp')), may hold values from -6 to 6
- cotangent: bfloat16 [65536, 1024], P(('dp', 'fsdp')), may hold values from -6 to 6
- weight: bfloat16 [8192, 1024], P('fsdp'), may hold values from -0.0625 to 0.0625
- feedback: float32 [8, 8192, 1024], P('dp', 'fsdp'), may hold values from -24 to 24
- q_factor: float32 [1024, 64], replicated, may hold values from -6 to 6
Outputs:
- input_grad: bfloat16 [65536, 8192], P(('dp', 'fsdp'))
- q_next: float32 [1024, 64], replicated
- feedback_next: float32 [8, 8192, 1024], P('dp', 'fsdp')
The draws below stay inside these ranges and needn't reach their ends.
All inputs are finite; a program needn't handle non-finite values.
Results may differ from the reference program's by a relative error of at most 0.012.
Values may be sent and summed in bfloat16 or wider, within the bound.
A program may use at most 128 MiB of HBM per device.

```python
import jax
import jax.numpy as jnp
from jax import lax

D = 8192
KVW = 1024
RANK = 64
TOK_DEV = 512
GROUPS = 8
TOKENS = 65536
N_DP = 8
N_FSDP = 16


def draw_feedback(key, part):
    keys = jax.random.split(key, 3)
    position = jnp.arange(D, dtype=jnp.float32) / D
    rising = jnp.exp(jnp.log(3.0) * position)
    row_scale = jnp.exp(jax.random.uniform(keys[0], (D,), minval=jnp.log(0.3), maxval=0.0)) * rising
    col_scale = jnp.exp(jax.random.uniform(keys[1], (KVW,), minval=jnp.log(0.5), maxval=jnp.log(2.0)))
    base = jax.random.truncated_normal(keys[2], -4.0, 4.0, (GROUPS, D, KVW))
    return (base * row_scale[None, :, None] * col_scale[None, None, :]).astype(jnp.float32)


def block_scale(rng, extent, shards, low, largest):
    def one(dim, blocks):
        heights = jax.random.uniform(jax.random.fold_in(jax.random.fold_in(rng, 6), dim), (blocks,), jnp.float32, low / len(shards), largest / len(shards))
        return jnp.repeat(jnp.exp(heights), extent[dim] // blocks).reshape((-1,) + (1,) * (len(extent) - dim - 1))

    factor_of = one(*shards[0])
    for cut in shards[1:]:
        factor_of = factor_of * one(*cut)
    return factor_of


def centred(rng, shape, deviation, reach, shards=(), kind=jnp.bfloat16):
    array = jax.random.normal(rng, shape, jnp.float32) * deviation
    if len(shards) > 0:
        array = block_scale(rng, shape, shards, -0.22, 0.18) * array
    return jnp.clip(array, min=-reach, max=reach).astype(kind)


def setup_inputs(seed: int = 0) -> dict:
    arg_keys = jax.random.split(jax.random.key(seed), 6)
    tokens = centred(arg_keys[0], (TOKENS, D), 1.0, 6.0, ((0, 128),))
    cotangent = centred(arg_keys[1], (TOKENS, KVW), 1.0, 6.0, ((0, 128),))
    weight = centred(arg_keys[2], (D, KVW), D ** -0.5, 0.0625, ((0, 16),))
    feedback = draw_feedback(jax.random.fold_in(arg_keys[5], 71), 0)
    q_factor = centred(arg_keys[4], (KVW, RANK), 1.0, 6.0, (), jnp.float32)
    return dict(tokens=tokens, cotangent=cotangent, weight=weight, feedback=feedback, q_factor=q_factor)


highest = lax.Precision.HIGHEST

def reference(tokens, cotangent, weight, feedback, q_factor):
    cot_groups = cotangent.reshape(N_DP, N_FSDP * TOK_DEV, KVW)
    weight_wide = weight.astype(jnp.float32)

    def project(cot_block):
        product = lax.dot_general(cot_block.astype(jnp.float32), weight_wide, (((1,), (1,)), ((), ())), precision=highest)
        return product.astype(jnp.bfloat16)
    input_grad = lax.map(project, cot_groups).reshape(N_DP * N_FSDP * TOK_DEV, D)
    tok_blocks = tokens.reshape(N_DP, N_FSDP, TOK_DEV, D)
    cot_blocks = cotangent.reshape(N_DP, N_FSDP, TOK_DEV, KVW)

    def add_block(total, item):
        product = lax.dot_general(item[0].astype(jnp.float32), item[1].astype(jnp.float32), (((0,), (0,)), ((), ())), precision=highest)
        rounded = lax.optimization_barrier(product.astype(jnp.bfloat16))
        return (total + rounded.astype(jnp.float32), None)

    def group_grad(pair):
        total, _ = lax.scan(add_block, jnp.zeros((D, KVW), jnp.float32), pair)
        return total
    grad_scale = 1.0 / (TOK_DEV * N_FSDP) ** 0.5
    grads = lax.map(group_grad, (tok_blocks, cot_blocks)) * grad_scale
    merged = feedback + grads
    mean_merged = lax.optimization_barrier(jnp.mean(merged, axis=0))
    factor_p = jnp.dot(mean_merged, q_factor, precision=highest)
    gram_sum = jnp.dot(factor_p.T, factor_p, precision=highest)
    lower_factor = jnp.linalg.cholesky(gram_sum)
    p_hat = lax.linalg.triangular_solve(lower_factor, factor_p.T, left_side=True, lower=True).T
    q_next = jnp.dot(mean_merged.T, p_hat, precision=highest)
    feedback_next = merged - jnp.dot(p_hat, q_next.T, precision=highest)[None]
    return (input_grad, q_next, feedback_next)
```

```python
import functools
import math

import jax
import jax.numpy as jnp
from jax import lax
from jax.experimental import pallas as pl
from jax.experimental.pallas import tpu as pltpu
from jax.sharding import PartitionSpec as P

MESH = pl.DeviceIdType.MESH
HIGHEST = lax.Precision.HIGHEST
F32 = jnp.float32
BF16 = jnp.bfloat16


def where_am_i():
    d = lax.axis_index("dp")
    f = lax.axis_index("fsdp")
    return d // 4, d % 4, f // 4, (f // 2) % 2, f % 2


def device(zh, y, x, zl, c):
    return (zh * 4 + y, x * 4 + zl * 2 + c)


def exact(left, right, dims):
    return lax.dot_general(left, right, (dims, ((), ())), precision=HIGHEST, preferred_element_type=F32)


def spread(src, slots, send_sem, recv_sem, me, targets):
    copies = []
    for k, target in enumerate(targets):
        copies.append(
            pltpu.make_async_remote_copy(
                src_ref=src(k),
                dst_ref=slots.at[me],
                send_sem=send_sem.at[k],
                recv_sem=recv_sem.at[k],
                device_id=target,
                device_id_type=MESH,
            )
        )
    for copy in copies:
        copy.start()
    return copies


def tail_kernel(
    grad_scale, feedback_ref, grad_ref, q_ref, qn_ref, fn_ref,
    merged, p_slots, g_slots, s_out, s1, s2, s3,
    p_send, p_recv, g_send, g_recv, s1_send, s1_recv, s2_send, s2_recv, s3_send, s3_recv,
):
    zh, y, x, zl, c = where_am_i()
    d = lax.axis_index("dp")
    f = lax.axis_index("fsdp")
    plane = x * 4 + y
    column = zh * 4 + zl * 2 + c

    group_of = [((d + k) % 8, f) for k in range(1, 8)]
    member_of = [(d, (f + k) % 16) for k in range(1, 16)]
    plane_at = [(plane + k) % 16 for k in range(1, 16)]
    plane_of = [device(zh, t % 4, t // 4, zl, c) for t in plane_at]
    column_at = [(column + k) % 8 for k in range(1, 8)]
    column_of = [device(t // 4, y, x, (t // 2) % 2, t % 2) for t in column_at]

    barrier = pltpu.get_barrier_semaphore()
    everyone = group_of + member_of + plane_of + column_of
    for target in everyone:
        pl.semaphore_signal(barrier, inc=1, device_id=target, device_id_type=MESH)

    merged[...] = feedback_ref[...] + grad_ref[...].astype(F32) * grad_scale
    p_slots[d] = exact(q_ref[...], merged[...], ((1,), (1,))).astype(BF16)
    pl.semaphore_wait(barrier, len(everyone))

    copies = spread(lambda k: p_slots.at[d], p_slots, p_send, p_recv, d, group_of)
    for copy in copies:
        copy.wait()
    total = p_slots[0].astype(F32)
    for k in range(1, 8):
        total = total + p_slots[k].astype(F32)
    factor = total * 0.125

    s_local = exact(factor, merged[...], ((1,), (0,))) * 0.125
    for i in range(4):
        for j in range(4):
            s_out[i * 4 + j] = s_local[16 * i : 16 * i + 16, 256 * j : 256 * j + 256]
    s1_copies = spread(lambda k: s_out.at[plane_at[k]], s1, s1_send, s1_recv, plane, plane_of)
    g_slots[f] = exact(factor, factor, ((1,), (1,)))
    g_copies = spread(lambda k: g_slots.at[f], g_slots, g_send, g_recv, f, member_of)
    s1[plane] = s_out[plane]
    for copy in s1_copies:
        copy.wait()
    part = s1[0]
    for k in range(1, 16):
        part = part + s1[k]
    s2[column] = part
    s2_copies = spread(lambda k: s2.at[column], s2, s2_send, s2_recv, column, column_of)

    for copy in g_copies:
        copy.wait()
    gram = g_slots[0]
    for k in range(1, 16):
        gram = gram + g_slots[k]
    row_id = lax.broadcasted_iota(jnp.int32, (64, 64), 0)
    lane_id = lax.broadcasted_iota(jnp.int32, (64, 64), 1)
    eye = jnp.where(row_id == lane_id, 1.0, 0.0).astype(F32)
    work = jnp.concatenate([eye, gram], axis=1)
    rows = lax.broadcasted_iota(jnp.int32, (64, 128), 0)

    def eliminate(work, k):
        pivot = jnp.broadcast_to(work[k : k + 1, 64 + k : 65 + k], (64, 128))
        column_k = jnp.broadcast_to(work[:, 64 + k : 65 + k], (64, 128))
        row_k = jnp.broadcast_to(work[k : k + 1, :], (64, 128))
        root = lax.rsqrt(pivot)
        root = root * (1.5 - 0.5 * pivot * root * root)
        scaled = row_k * root
        below = work - (column_k * root) * scaled
        return jnp.where(rows > k, below, jnp.where(rows == k, scaled, work))

    for k in range(16):
        work = eliminate(work, k)

    for copy in s2_copies:
        copy.wait()
    part = s2[0]
    for k in range(1, 8):
        part = part + s2[k]
    s3[plane] = part
    s3_copies = spread(lambda k: s3.at[plane], s3, s3_send, s3_recv, plane, plane_of)

    for k in range(16, 64):
        work = eliminate(work, k)
    inverse = work[:, :64]
    p_hat = jnp.transpose(exact(inverse, factor, ((1,), (0,))))

    for copy in s3_copies:
        copy.wait()
    s_total = jnp.concatenate(
        [jnp.concatenate([s3[i * 4 + j] for j in range(4)], axis=1) for i in range(4)], axis=0
    )
    q_next = exact(inverse, s_total, ((1,), (0,)))
    qn_ref[...] = q_next
    fn_ref[...] = merged[...] - exact(p_hat, q_next, ((1,), (0,)))


def tail(feedback, grad_rows, q_t, grad_scale):
    rows, width = feedback.shape
    rank = q_t.shape[0]
    vmem = pl.BlockSpec(memory_space=pltpu.VMEM)
    dma = pltpu.SemaphoreType.DMA
    return pl.pallas_call(
        functools.partial(tail_kernel, grad_scale),
        out_shape=(
            jax.ShapeDtypeStruct((rank, width), F32),
            jax.ShapeDtypeStruct((rows, width), F32),
        ),
        in_specs=[vmem] * 3,
        out_specs=(vmem, vmem),
        scratch_shapes=[
            pltpu.VMEM((rows, width), F32),
            pltpu.VMEM((8, rank, rows), BF16),
            pltpu.VMEM((16, rank, rank), F32),
            pltpu.VMEM((16, 16, 256), F32),
            pltpu.VMEM((16, 16, 256), F32),
            pltpu.VMEM((8, 16, 256), F32),
            pltpu.VMEM((16, 16, 256), F32),
            dma((7,)), dma((7,)), dma((15,)), dma((15,)), dma((15,)), dma((15,)),
            dma((7,)), dma((7,)), dma((15,)), dma((15,)),
        ],
        compiler_params=pltpu.CompilerParams(
            collective_id=1, has_side_effects=True, vmem_limit_bytes=48 * 1024 * 1024
        ),
        name="tail",
    )(feedback, grad_rows, q_t)


def per_device(tokens, cotangent, weight, feedback, q_factor):
    members = lax.axis_size("fsdp")
    grad_scale = 1.0 / math.sqrt(tokens.shape[0] * members)
    product = lax.dot_general(
        cotangent,
        lax.all_gather(weight, "fsdp", axis=0, tiled=True),
        (((1,), (1,)), ((), ())),
        preferred_element_type=F32,
    )
    input_grad = product.astype(BF16)
    grad_rows = lax.psum_scatter(
        lax.dot_general(
            tokens, cotangent, (((0,), (0,)), ((), ())), preferred_element_type=F32
        ).astype(BF16),
        "fsdp",
        scatter_dimension=0,
        tiled=True,
    )
    q_next, feedback_next = tail(feedback[0], grad_rows, q_factor.T, grad_scale)
    return (input_grad, q_next.T, feedback_next[None])


def solution(mesh):
    placed = (
        P(("dp", "fsdp"), None),
        P(("dp", "fsdp"), None),
        P("fsdp", None),
        P("dp", "fsdp", None),
        P(),
    )
    return jax.shard_map(
        per_device,
        mesh=mesh,
        in_specs=placed,
        out_specs=(P(("dp", "fsdp"), None), P(), P("dp", "fsdp", None)),
        check_vma=False,
    )
```

```python
import functools
import math

import jax
import jax.numpy as jnp
from jax import lax
from jax.experimental import pallas as pl
from jax.experimental.pallas import tpu as pltpu
from jax.sharding import PartitionSpec as P

MESH = pl.DeviceIdType.MESH
HIGHEST = lax.Precision.HIGHEST
F32 = jnp.float32
BF16 = jnp.bfloat16


def where_am_i():
    d = lax.axis_index("dp")
    f = lax.axis_index("fsdp")
    return d // 4, d % 4, f // 4, (f // 2) % 2, f % 2


def device(zh, y, x, zl, c):
    return (zh * 4 + y, x * 4 + zl * 2 + c)


def exact(left, right, dims):
    return lax.dot_general(left, right, (dims, ((), ())), precision=HIGHEST, preferred_element_type=F32)


def spread(src, slots, send_sem, recv_sem, me, targets):
    copies = []
    for k, target in enumerate(targets):
        copies.append(
            pltpu.make_async_remote_copy(
                src_ref=src(k),
                dst_ref=slots.at[me],
                send_sem=send_sem.at[k],
                recv_sem=recv_sem.at[k],
                device_id=target,
                device_id_type=MESH,
            )
        )
    for copy in copies:
        copy.start()
    return copies


def tail_kernel(
    merged, q_ref, qn_ref, fn_ref,
    p_slots, g_slots, s_out, s1, s2, s3,
    p_send, p_recv, g_send, g_recv, s1_send, s1_recv, s2_send, s2_recv, s3_send, s3_recv,
):
    zh, y, x, zl, c = where_am_i()
    d = lax.axis_index("dp")
    f = lax.axis_index("fsdp")
    plane = x * 4 + y
    column = zh * 4 + zl * 2 + c

    group_of = [((d + k) % 8, f) for k in range(1, 8)]
    member_of = [(d, (f + k) % 16) for k in range(1, 16)]
    plane_at = [(plane + k) % 16 for k in range(1, 16)]
    plane_of = [device(zh, t % 4, t // 4, zl, c) for t in plane_at]
    column_at = [(column + k) % 8 for k in range(1, 8)]
    column_of = [device(t // 4, y, x, (t // 2) % 2, t % 2) for t in column_at]

    barrier = pltpu.get_barrier_semaphore()
    everyone = group_of + member_of + plane_of + column_of
    for target in everyone:
        pl.semaphore_signal(barrier, inc=1, device_id=target, device_id_type=MESH)

    p_slots[d] = exact(q_ref[...], merged[...], ((1,), (1,))).astype(BF16)
    pl.semaphore_wait(barrier, len(everyone))

    copies = spread(lambda k: p_slots.at[d], p_slots, p_send, p_recv, d, group_of)
    for copy in copies:
        copy.wait()
    total = p_slots[0].astype(F32)
    for k in range(1, 8):
        total = total + p_slots[k].astype(F32)
    factor = total * 0.125

    s_local = exact(factor, merged[...], ((1,), (0,))) * 0.125
    for i in range(4):
        for j in range(4):
            s_out[i * 4 + j] = s_local[16 * i : 16 * i + 16, 256 * j : 256 * j + 256]
    s1_copies = spread(lambda k: s_out.at[plane_at[k]], s1, s1_send, s1_recv, plane, plane_of)
    g_slots[f] = exact(factor, factor, ((1,), (1,)))
    g_copies = spread(lambda k: g_slots.at[f], g_slots, g_send, g_recv, f, member_of)
    s1[plane] = s_out[plane]
    for copy in s1_copies:
        copy.wait()
    part = s1[0]
    for k in range(1, 16):
        part = part + s1[k]
    s2[column] = part
    s2_copies = spread(lambda k: s2.at[column], s2, s2_send, s2_recv, column, column_of)

    for copy in g_copies:
        copy.wait()
    gram = g_slots[0]
    for k in range(1, 16):
        gram = gram + g_slots[k]
    row_id = lax.broadcasted_iota(jnp.int32, (64, 64), 0)
    lane_id = lax.broadcasted_iota(jnp.int32, (64, 64), 1)
    eye = jnp.where(row_id == lane_id, 1.0, 0.0).astype(F32)
    work = jnp.concatenate([eye, gram], axis=1)
    rows = lax.broadcasted_iota(jnp.int32, (64, 128), 0)

    def eliminate(work, k):
        pivot = jnp.broadcast_to(work[k : k + 1, 64 + k : 65 + k], (64, 128))
        column_k = jnp.broadcast_to(work[:, 64 + k : 65 + k], (64, 128))
        row_k = jnp.broadcast_to(work[k : k + 1, :], (64, 128))
        root = lax.rsqrt(pivot)
        root = root * (1.5 - 0.5 * pivot * root * root)
        scaled = row_k * root
        below = work - (column_k * root) * scaled
        return jnp.where(rows > k, below, jnp.where(rows == k, scaled, work))

    for k in range(16):
        work = eliminate(work, k)

    for copy in s2_copies:
        copy.wait()
    part = s2[0]
    for k in range(1, 8):
        part = part + s2[k]
    s3[plane] = part
    s3_copies = spread(lambda k: s3.at[plane], s3, s3_send, s3_recv, plane, plane_of)

    for k in range(16, 64):
        work = eliminate(work, k)
    inverse = work[:, :64]
    p_hat = jnp.transpose(exact(inverse, factor, ((1,), (0,))))

    for copy in s3_copies:
        copy.wait()
    s_total = jnp.concatenate(
        [jnp.concatenate([s3[i * 4 + j] for j in range(4)], axis=1) for i in range(4)], axis=0
    )
    q_next = exact(inverse, s_total, ((1,), (0,)))
    qn_ref[...] = q_next
    fn_ref[...] = merged[...] - exact(p_hat, q_next, ((1,), (0,)))


def tail(merged, q_t):
    rows, width = merged.shape
    rank = q_t.shape[0]
    vmem = pl.BlockSpec(memory_space=pltpu.VMEM)
    dma = pltpu.SemaphoreType.DMA
    return pl.pallas_call(
        tail_kernel,
        out_shape=(
            jax.ShapeDtypeStruct((rank, width), F32),
            jax.ShapeDtypeStruct((rows, width), F32),
        ),
        in_specs=[vmem] * 2,
        out_specs=(vmem, vmem),
        scratch_shapes=[
            pltpu.VMEM((8, rank, rows), BF16),
            pltpu.VMEM((16, rank, rank), F32),
            pltpu.VMEM((16, 16, 256), F32),
            pltpu.VMEM((16, 16, 256), F32),
            pltpu.VMEM((8, 16, 256), F32),
            pltpu.VMEM((16, 16, 256), F32),
            dma((7,)), dma((7,)), dma((15,)), dma((15,)), dma((15,)), dma((15,)),
            dma((7,)), dma((7,)), dma((15,)), dma((15,)),
        ],
        compiler_params=pltpu.CompilerParams(
            collective_id=1, has_side_effects=True, vmem_limit_bytes=48 * 1024 * 1024
        ),
        name="tail",
    )(merged, q_t)


ORDER = [(2, 1), (1, 1), (3, 1), (0, 1), (2, 0), (1, 0), (3, 0), (0, 0)]
SLOT = {relative: o for o, relative in enumerate(ORDER)}
Y_UP = [(0, 0), (2, 0), (1, 1), (3, 1)]
Y_DOWN = [(3, 0), (1, 0), (0, 1), (2, 1)]
N_COPIES = 96


class Copies:
    def __init__(self, send, recv):
        self.send, self.recv, self.used, self.all = send, recv, 0, {}

    def start(self, name, src, dst, target):
        copy = pltpu.make_async_remote_copy(
            src_ref=src,
            dst_ref=dst,
            send_sem=self.send.at[self.used],
            recv_sem=self.recv.at[self.used],
            device_id=target,
            device_id_type=MESH,
        )
        self.used += 1
        copy.start()
        self.all[name] = copy

    def arrived(self, name):
        self.all[name].wait_recv()

    def finish(self):
        for copy in self.all.values():
            copy.wait_send()


def grads_kernel(
    grad_scale, tokens, cotangent, weight, feedback, input_grad, merged,
    tok, cot, part, hop, side, z_last, z_send, z_first, w_all, staged,
    send, recv, load_sem, store_sem,
):
    zh, y, x, zl, c = where_am_i()
    half = y % 2
    mate = device(zh, y, x, zl, 1 - c)
    x_up, x_down = device(zh, y, (x + 1) % 4, zl, c), device(zh, y, (x + 3) % 4, zl, c)
    y_up, y_down = device(zh, (y + 1) % 4, x, zl, c), device(zh, (y + 3) % 4, x, zl, c)
    z_pair, z_across = device(zh, y, x, 1 - zl, c), device(1 - zh, y, x, 1 - zl, c)
    partners = [mate, x_up, x_down, y_up, y_down, z_pair, z_across]

    def first_row(relative, core):
        rx, rz = relative
        return (((x + rx) % 4) * 4 + ((zl + rz) % 2) * 2 + core) * 512

    barrier = pltpu.get_barrier_semaphore()
    for target in partners:
        pl.semaphore_signal(barrier, inc=1, device_id=target, device_id_type=MESH)
    loads = [pltpu.make_async_copy(cotangent, cot.at[0:512], load_sem.at[8])]
    for o, relative in enumerate(ORDER):
        columns = pl.ds(pl.multiple_of(first_row(relative, c), 512), 512)
        loads.append(pltpu.make_async_copy(tokens.at[:, columns], tok.at[o, 0:512], load_sem.at[o]))
    for load in loads:
        load.start()
    pl.semaphore_wait(barrier, len(partners))

    go = Copies(send, recv)
    go.start("cot", cotangent, cot.at[512:1024], mate)
    for o, relative in enumerate(ORDER):
        columns = pl.ds(pl.multiple_of(first_row(relative, 1 - c), 512), 512)
        go.start(("tok", o), tokens.at[:, columns], tok.at[o, 512:1024], mate)

    my_half = weight.at[pl.ds(pl.multiple_of(half * 256, 256), 256)]
    own_half = pltpu.make_async_copy(my_half, w_all.at[SLOT[0, 0], 0], load_sem.at[9])
    own_half.start()
    go.start(("wx", 3), my_half, w_all.at[SLOT[3, 0], 0], x_up)
    go.start(("wx", 1), my_half, w_all.at[SLOT[1, 0], 0], x_down)
    go.start(("wz", 0), my_half, w_all.at[SLOT[0, 1], 0], z_across)
    go.start(("wy", (0, 0)), my_half, w_all.at[SLOT[0, 0], 1], y_up)

    def weight_y(relative):
        target = y_up if relative in Y_UP else y_down
        go.start(("wy", relative), w_all.at[SLOT[relative], 0], w_all.at[SLOT[relative], 1], target)

    def weight_x():
        go.arrived(("wx", 3))
        go.start(("wf", 0), w_all.at[SLOT[3, 0], 0, 0:128], w_all.at[SLOT[2, 0], 0, 0:128], x_up)
        go.start(("wz", 3), w_all.at[SLOT[3, 0], 0], w_all.at[SLOT[3, 1], 0], z_across)
        weight_y((3, 0))
        go.arrived(("wx", 1))
        go.start(("wf", 1), w_all.at[SLOT[1, 0], 0, 128:256], w_all.at[SLOT[2, 0], 0, 128:256], x_down)
        go.start(("wz", 1), w_all.at[SLOT[1, 0], 0], w_all.at[SLOT[1, 1], 0], z_across)
        weight_y((1, 0))

    def weight_opposite():
        go.arrived(("wf", 0))
        go.arrived(("wf", 1))
        go.start(("wz", 2), w_all.at[SLOT[2, 0], 0], w_all.at[SLOT[2, 1], 0], z_across)
        weight_y((2, 0))

    def weight_z(rx):
        go.arrived(("wz", rx))
        weight_y((rx, 1))

    stores = []

    def project(relative, which):
        n = len(stores)
        slot = SLOT[relative]

        @pl.loop(0, 4)
        def _(i):
            rows = pl.ds(pl.multiple_of(i * 256, 256), 256)
            staged[n, rows] = lax.dot_general(
                cot[rows], w_all[slot, which], (((1,), (1,)), ((), ())), preferred_element_type=F32
            ).astype(BF16)

        column = first_row(relative, c) + (half if which == 0 else 1 - half) * 256
        columns = pl.ds(pl.multiple_of(column, 256), 256)
        store = pltpu.make_async_copy(staged.at[n, 0:512], input_grad.at[:, columns], store_sem.at[n])
        store.start()
        stores.append(store)
        go.start(("out", n), staged.at[n, 512:1024], input_grad.at[:, columns], mate)

    def project_y(relative):
        go.arrived(("wy", relative))
        project(relative, 1)

    def partial(o):
        loads[1 + o].wait()
        go.arrived(("tok", o))

        @pl.loop(0, 2)
        def _(i):
            rows = pl.ds(pl.multiple_of(i * 256, 256), 256)
            part[o, rows] = lax.dot_general(
                tok[o, :, rows], cot[...], (((0,), (0,)), ((), ())), preferred_element_type=F32
            ).astype(BF16)

    START = [0, 0, 512]
    ACROSS = [1, 0, 0]

    def columns_of(s, which):
        return pl.ds(START[s] + 256 * which, 256)

    def opposite(s):
        src = part.at[SLOT[2, ACROSS[s]]]
        go.start(("hop", s, 0), src.at[:, columns_of(s, 0)], hop.at[s, 0], x_up)
        go.start(("hop", s, 1), src.at[:, columns_of(s, 1)], hop.at[s, 1], x_down)

    def beside_up(s):
        src = part.at[SLOT[1, ACROSS[s]]]
        go.start(("side", s, 0, 1), src.at[:, columns_of(s, 1)], side.at[s, 0, :, 256:512], x_up)

    def beside_down(s):
        src = part.at[SLOT[3, ACROSS[s]]]
        go.start(("side", s, 1, 0), src.at[:, columns_of(s, 0)], side.at[s, 1, :, 0:256], x_down)

    def add_into(dst, dst_columns, src, src_columns):
        @pl.loop(0, 4)
        def _(i):
            rows = pl.ds(pl.multiple_of(i * 128, 128), 128)
            dst[rows, dst_columns] = (
                dst[rows, dst_columns].astype(F32) + src[rows, src_columns].astype(F32)
            ).astype(BF16)

    def pass_on(s):
        for which, rx, target in ((0, 1, x_up), (1, 3, x_down)):
            go.arrived(("hop", s, which))
            mine = part.at[SLOT[rx, ACROSS[s]]]
            add_into(mine, columns_of(s, which), hop.at[s, which], pl.ds(0, 256))
            go.start(
                ("side", s, which, which), mine.at[:, columns_of(s, which)],
                side.at[s, which, :, 256 * which : 256 * which + 256], target,
            )

    def sides_arrived(s):
        for which in range(2):
            for columns in range(2):
                go.arrived(("side", s, which, columns))

    def z_exchange(rx):
        go.start(("z1", rx), part.at[SLOT[rx, 1], :, 512:1024], z_first.at[rx], z_pair)

    def z_sum(rx):
        go.arrived(("z1", rx))
        add_into(part.at[SLOT[rx, 0]], pl.ds(512, 512), z_first.at[rx], pl.ds(0, 512))

    def finish_across():
        sides_arrived(0)

        @pl.loop(0, 4)
        def _(i):
            rows = pl.ds(pl.multiple_of(i * 128, 128), 128)
            z_send[rows] = (
                part[SLOT[0, 1], rows, 0:512].astype(F32)
                + side[0, 0, rows].astype(F32)
                + side[0, 1, rows].astype(F32)
            ).astype(BF16)

        go.start("z2", z_send, z_last, z_pair)

    def finish_here():
        sides_arrived(1)
        go.arrived("z2")

        @pl.loop(0, 4)
        def _(i):
            rows = pl.ds(pl.multiple_of(i * 128, 128), 128)
            total = (
                part[SLOT[0, 0], rows, 0:512].astype(F32)
                + side[1, 0, rows].astype(F32)
                + side[1, 1, rows].astype(F32)
                + z_last[rows].astype(F32)
            )
            merged[rows, 0:512] = feedback[rows, 0:512] + total * grad_scale

    def finish_second():
        sides_arrived(2)
        go.arrived(("z1", 0))

        @pl.loop(0, 4)
        def _(i):
            rows = pl.ds(pl.multiple_of(i * 128, 128), 128)
            total = (
                part[SLOT[0, 0], rows, 512:1024].astype(F32)
                + side[2, 0, rows].astype(F32)
                + side[2, 1, rows].astype(F32)
                + z_first[0, rows].astype(F32)
            )
            merged[rows, 512:1024] = feedback[rows, 512:1024] + total * grad_scale

    loads[0].wait()
    go.arrived("cot")
    partial(0)
    opposite(0)
    z_exchange(2)
    partial(1)
    beside_up(0)
    z_exchange(1)
    partial(2)
    beside_down(0)
    z_exchange(3)
    partial(3)
    z_exchange(0)
    partial(4)
    opposite(1)
    partial(5)
    beside_up(1)
    partial(6)
    beside_down(1)
    pass_on(0)
    partial(7)
    weight_x()
    own_half.wait()
    project((0, 0), 0)
    project_y((0, 0))
    z_sum(2)
    opposite(2)
    weight_z(0)
    project((0, 1), 0)
    project((3, 0), 0)
    pass_on(1)
    weight_opposite()
    project((1, 0), 0)
    z_sum(1)
    beside_up(2)
    project((2, 0), 0)
    weight_z(3)
    finish_across()
    project((3, 1), 0)
    project_y((3, 0))
    weight_z(1)
    z_sum(3)
    beside_down(2)
    project((1, 1), 0)
    pass_on(2)
    project_y((1, 0))
    weight_z(2)
    project((2, 1), 0)
    project_y((2, 0))
    project_y((0, 1))
    project_y((3, 1))
    finish_here()
    project_y((1, 1))
    project_y((2, 1))
    finish_second()
    for n in range(16):
        go.arrived(("out", n))
        stores[n].wait()
    go.finish()


def grads(tokens, cotangent, weight, feedback, grad_scale):
    rows, width = feedback.shape
    vmem = pl.BlockSpec(memory_space=pltpu.VMEM)
    hbm = pl.BlockSpec(memory_space=pl.ANY)
    dma = pltpu.SemaphoreType.DMA
    return pl.pallas_call(
        functools.partial(grads_kernel, grad_scale),
        out_shape=(
            jax.ShapeDtypeStruct(tokens.shape, BF16),
            jax.ShapeDtypeStruct((rows, width), F32),
        ),
        in_specs=[hbm, hbm, hbm, vmem],
        out_specs=(hbm, vmem),
        scratch_shapes=[
            pltpu.VMEM((8, 1024, 512), BF16),
            pltpu.VMEM((1024, 1024), BF16),
            pltpu.VMEM((8, 512, 1024), BF16),
            pltpu.VMEM((3, 2, 512, 256), BF16),
            pltpu.VMEM((3, 2, 512, 512), BF16),
            pltpu.VMEM((512, 512), BF16),
            pltpu.VMEM((512, 512), BF16),
            pltpu.VMEM((4, 512, 512), BF16),
            pltpu.VMEM((8, 2, 256, 1024), BF16),
            pltpu.VMEM((16, 1024, 256), BF16),
            dma((N_COPIES,)), dma((N_COPIES,)), dma((10,)), dma((16,)),
        ],
        compiler_params=pltpu.CompilerParams(
            collective_id=2, has_side_effects=True, vmem_limit_bytes=60 * 1024 * 1024
        ),
        name="grads",
    )(tokens, cotangent, weight, feedback)


def per_device(tokens, cotangent, weight, feedback, q_factor):
    members = lax.axis_size("fsdp")
    grad_scale = 1.0 / math.sqrt(tokens.shape[0] * members)
    input_grad, merged = grads(tokens, cotangent, weight, feedback[0], grad_scale)
    q_next, feedback_next = tail(merged, q_factor.T)
    return (input_grad, q_next.T, feedback_next[None])


def solution(mesh):
    placed = (
        P(("dp", "fsdp"), None),
        P(("dp", "fsdp"), None),
        P("fsdp", None),
        P("dp", "fsdp", None),
        P(),
    )
    return jax.shard_map(
        per_device,
        mesh=mesh,
        in_specs=placed,
        out_specs=(P(("dp", "fsdp"), None), P(), P("dp", "fsdp", None)),
        check_vma=False,
    )
```

```python
import functools
import math

import jax
import jax.numpy as jnp
from jax import lax
from jax.experimental import pallas as pl
from jax.experimental.pallas import tpu as pltpu
from jax.sharding import PartitionSpec as P

MESH = pl.DeviceIdType.MESH
HIGHEST = lax.Precision.HIGHEST
F32 = jnp.float32
BF16 = jnp.bfloat16


def where_am_i():
    d = lax.axis_index("dp")
    f = lax.axis_index("fsdp")
    return d // 4, d % 4, f // 4, (f // 2) % 2, f % 2


def device(zh, y, x, zl, c):
    return (zh * 4 + y, x * 4 + zl * 2 + c)


def exact(left, right, dims):
    return lax.dot_general(left, right, (dims, ((), ())), precision=HIGHEST, preferred_element_type=F32)


def spread(copies, name, src, slots, me, targets):
    for k, target in enumerate(targets):
        copies.start((name, k), src(k), slots.at[me], target)


def gathered(copies, name, targets):
    for k in range(len(targets)):
        copies.arrived((name, k))


def total_of(slots, n):
    total = slots[0].astype(F32)
    for k in range(1, n):
        total = total + slots[k].astype(F32)
    return total


def eliminate(work, k, row_id):
    group, first = k // 8, k % 8
    columns = [jnp.broadcast_to(work[:, :, 64 + k + j : 65 + k + j], (8, 8, 128)) for j in range(4)]
    rows = [jnp.broadcast_to(work[group, first + j : first + j + 1, :], (8, 128)) for j in range(4)]
    pivot = {}
    for j in range(4):
        for i in range(j, 4):
            pivot[i, j] = jnp.broadcast_to(columns[j][group, first + i : first + i + 1, :], (8, 128))
    for j in range(4):
        inverse = 1.0 / pivot[j, j]
        multiplier = columns[j] * inverse
        for i in range(j + 1, 4):
            columns[i] = columns[i] - multiplier * pivot[i, j]
            scale = pivot[i, j] * inverse
            rows[i] = rows[i] - scale * rows[j]
            for m in range(i, 4):
                pivot[m, i] = pivot[m, i] - scale * pivot[m, j]
        work = work - jnp.where(row_id > k + j, multiplier, 0.0) * rows[j]
    return work


ORDER = [(2, 1), (1, 1), (3, 1), (0, 1), (2, 0), (1, 0), (3, 0), (0, 0)]
SLOT = {relative: o for o, relative in enumerate(ORDER)}
Y_UP = [(0, 0), (3, 0), (2, 0), (1, 1)]
N_COPIES = 144


class Copies:
    def __init__(self, send, recv):
        self.send, self.recv, self.used, self.all = send, recv, 0, {}

    def start(self, name, src, dst, target):
        copy = pltpu.make_async_remote_copy(
            src_ref=src,
            dst_ref=dst,
            send_sem=self.send.at[self.used],
            recv_sem=self.recv.at[self.used],
            device_id=target,
            device_id_type=MESH,
        )
        self.used += 1
        copy.start()
        self.all[name] = copy

    def arrived(self, name):
        self.all[name].wait_recv()

    def finish(self):
        for copy in self.all.values():
            copy.wait_send()


def step_kernel(
    grad_scale, tokens, cotangent, weight, feedback, q_ref, input_grad, merged, p_hat_ref, q_next_ref,
    tok, cot, part, hop, side, z_last, z_send, z_first, w_all,
    pa_slots, pb_slots, g_slots, s_out, s1, s2, s3,
    send, recv, load_sem, store_sem,
):
    zh, y, x, zl, c = where_am_i()
    half = y % 2
    mate = device(zh, y, x, zl, 1 - c)
    x_up, x_down = device(zh, y, (x + 1) % 4, zl, c), device(zh, y, (x + 3) % 4, zl, c)
    y_up, y_down = device(zh, (y + 1) % 4, x, zl, c), device(zh, (y + 3) % 4, x, zl, c)
    z_pair, z_across = device(zh, y, x, 1 - zl, c), device(1 - zh, y, x, 1 - zl, c)
    d = lax.axis_index("dp")
    f = lax.axis_index("fsdp")
    plane = x * 4 + y
    column = zh * 4 + zl * 2 + c
    y_of = [device(zh, (y + k) % 4, x, zl, c) for k in range(1, 4)]
    z_of = [device(1 - zh, y, x, zl, c)]
    member_of = [(d, (f + k) % 16) for k in range(1, 16)]
    plane_at = [(plane + k) % 16 for k in range(1, 16)]
    plane_of = [device(zh, t % 4, t // 4, zl, c) for t in plane_at]
    column_at = [(column + k) % 8 for k in range(1, 8)]
    column_of = [device(t // 4, y, x, (t // 2) % 2, t % 2) for t in column_at]
    partners = [mate, x_up, x_down, y_up, y_down, z_pair, z_across]
    partners = partners + y_of + z_of + member_of + plane_of + column_of

    def first_row(relative, core):
        rx, rz = relative
        return (((x + rx) % 4) * 4 + ((zl + rz) % 2) * 2 + core) * 512

    barrier = pltpu.get_barrier_semaphore()
    for target in partners:
        pl.semaphore_signal(barrier, inc=1, device_id=target, device_id_type=MESH)
    loads = [pltpu.make_async_copy(cotangent, cot.at[0:512], load_sem.at[8])]
    for o, relative in enumerate(ORDER):
        columns = pl.ds(pl.multiple_of(first_row(relative, c), 512), 512)
        loads.append(pltpu.make_async_copy(tokens.at[:, columns], tok.at[o, 0:512], load_sem.at[o]))
    for load in loads:
        load.start()
    pl.semaphore_wait(barrier, len(partners))

    go = Copies(send, recv)
    go.start("cot", cotangent, cot.at[512:1024], mate)
    for o, relative in enumerate(ORDER):
        columns = pl.ds(pl.multiple_of(first_row(relative, 1 - c), 512), 512)
        go.start(("tok", o), tokens.at[:, columns], tok.at[o, 512:1024], mate)

    my_half = weight.at[pl.ds(pl.multiple_of(half * 256, 256), 256)]
    own_half = pltpu.make_async_copy(my_half, w_all.at[SLOT[0, 0], 0], load_sem.at[9])
    own_half.start()
    go.start(("wx", 3), my_half, w_all.at[SLOT[3, 0], 0], x_up)
    go.start(("wx", 1), my_half, w_all.at[SLOT[1, 0], 0], x_down)
    go.start(("wz", 0), my_half, w_all.at[SLOT[0, 1], 0], z_across)
    go.start(("wy", (0, 0)), my_half, w_all.at[SLOT[0, 0], 1], y_up)

    def weight_y(relative):
        target = y_up if relative in Y_UP else y_down
        go.start(("wy", relative), w_all.at[SLOT[relative], 0], w_all.at[SLOT[relative], 1], target)

    def weight_x():
        go.arrived(("wx", 3))
        go.start(("wf", 0), w_all.at[SLOT[3, 0], 0, 0:128], w_all.at[SLOT[2, 0], 0, 0:128], x_up)
        go.start(("wz", 3), w_all.at[SLOT[3, 0], 0], w_all.at[SLOT[3, 1], 0], z_across)
        weight_y((3, 0))
        go.arrived(("wx", 1))
        go.start(("wf", 1), w_all.at[SLOT[1, 0], 0, 128:256], w_all.at[SLOT[2, 0], 0, 128:256], x_down)
        go.start(("wz", 1), w_all.at[SLOT[1, 0], 0], w_all.at[SLOT[1, 1], 0], z_across)
        weight_y((1, 0))

    def weight_opposite():
        go.arrived(("wf", 0))
        go.arrived(("wf", 1))
        go.start(("wz", 2), w_all.at[SLOT[2, 0], 0], w_all.at[SLOT[2, 1], 0], z_across)
        weight_y((2, 0))

    def weight_z(rx):
        go.arrived(("wz", rx))
        weight_y((rx, 1))

    stores = []

    def project(relative, which):
        n = len(stores)
        slot = SLOT[relative]

        @pl.loop(0, 4)
        def _(i):
            rows = pl.ds(pl.multiple_of(i * 256, 256), 256)
            tok[slot, rows, 256 * which : 256 * which + 256] = lax.dot_general(
                cot[rows], w_all[slot, which], (((1,), (1,)), ((), ())), preferred_element_type=F32
            ).astype(BF16)

        column = first_row(relative, c) + (half if which == 0 else 1 - half) * 256
        columns = pl.ds(pl.multiple_of(column, 256), 256)
        made = tok.at[slot, :, 256 * which : 256 * which + 256]
        store = pltpu.make_async_copy(made.at[0:512], input_grad.at[:, columns], store_sem.at[n])
        store.start()
        stores.append(store)
        go.start(("out", n), made.at[512:1024], input_grad.at[:, columns], mate)

    def project_y(relative):
        go.arrived(("wy", relative))
        project(relative, 1)

    def partial(o):
        loads[1 + o].wait()
        go.arrived(("tok", o))

        @pl.loop(0, 2)
        def _(i):
            rows = pl.ds(pl.multiple_of(i * 256, 256), 256)
            part[o, rows] = lax.dot_general(
                tok[o, :, rows], cot[...], (((0,), (0,)), ((), ())), preferred_element_type=F32
            ).astype(BF16)

    START = [0, 0, 512]
    ACROSS = [1, 0, 0]

    def columns_of(s, which):
        return pl.ds(START[s] + 256 * which, 256)

    def opposite(s):
        src = part.at[SLOT[2, ACROSS[s]]]
        go.start(("hop", s, 0), src.at[:, columns_of(s, 0)], hop.at[s, 0], x_up)
        go.start(("hop", s, 1), src.at[:, columns_of(s, 1)], hop.at[s, 1], x_down)

    def beside_up(s):
        src = part.at[SLOT[1, ACROSS[s]]]
        go.start(("side", s, 0, 1), src.at[:, columns_of(s, 1)], side.at[s, 0, :, 256:512], x_up)

    def beside_down(s):
        src = part.at[SLOT[3, ACROSS[s]]]
        go.start(("side", s, 1, 0), src.at[:, columns_of(s, 0)], side.at[s, 1, :, 0:256], x_down)

    def add_into(dst, dst_columns, src, src_columns):
        @pl.loop(0, 4)
        def _(i):
            rows = pl.ds(pl.multiple_of(i * 128, 128), 128)
            dst[rows, dst_columns] = (
                dst[rows, dst_columns].astype(F32) + src[rows, src_columns].astype(F32)
            ).astype(BF16)

    def pass_on(s):
        for which, rx, target in ((0, 1, x_up), (1, 3, x_down)):
            go.arrived(("hop", s, which))
            mine = part.at[SLOT[rx, ACROSS[s]]]
            add_into(mine, columns_of(s, which), hop.at[s, which], pl.ds(0, 256))
            go.start(
                ("side", s, which, which), mine.at[:, columns_of(s, which)],
                side.at[s, which, :, 256 * which : 256 * which + 256], target,
            )

    def sides_arrived(s):
        for which in range(2):
            for columns in range(2):
                go.arrived(("side", s, which, columns))

    def z_exchange(rx):
        go.start(("z1", rx), part.at[SLOT[rx, 1], :, 512:1024], z_first.at[rx], z_pair)

    def z_sum(rx):
        go.arrived(("z1", rx))
        add_into(part.at[SLOT[rx, 0]], pl.ds(512, 512), z_first.at[rx], pl.ds(0, 512))

    def finish_across():
        sides_arrived(0)

        @pl.loop(0, 4)
        def _(i):
            rows = pl.ds(pl.multiple_of(i * 128, 128), 128)
            z_send[rows] = (
                part[SLOT[0, 1], rows, 0:512].astype(F32)
                + side[0, 0, rows].astype(F32)
                + side[0, 1, rows].astype(F32)
            ).astype(BF16)

        go.start("z2", z_send, z_last, z_pair)

    def finish_here():
        sides_arrived(1)
        go.arrived("z2")

        @pl.loop(0, 4)
        def _(i):
            rows = pl.ds(pl.multiple_of(i * 128, 128), 128)
            total = (
                part[SLOT[0, 0], rows, 0:512].astype(F32)
                + side[1, 0, rows].astype(F32)
                + side[1, 1, rows].astype(F32)
                + z_last[rows].astype(F32)
            )
            merged[rows, 0:512] = feedback[rows, 0:512] + total * grad_scale

    def finish_second():
        sides_arrived(2)
        go.arrived(("z1", 0))

        @pl.loop(0, 4)
        def _(i):
            rows = pl.ds(pl.multiple_of(i * 128, 128), 128)
            total = (
                part[SLOT[0, 0], rows, 512:1024].astype(F32)
                + side[2, 0, rows].astype(F32)
                + side[2, 1, rows].astype(F32)
                + z_first[0, rows].astype(F32)
            )
            merged[rows, 512:1024] = feedback[rows, 512:1024] + total * grad_scale

    loads[0].wait()
    go.arrived("cot")
    partial(0)
    opposite(0)
    z_exchange(2)
    partial(1)
    beside_up(0)
    z_exchange(1)
    partial(2)
    beside_down(0)
    z_exchange(3)
    partial(3)
    z_exchange(0)
    weight_x()
    partial(4)
    opposite(1)
    weight_z(0)
    partial(5)
    beside_up(1)
    pass_on(0)
    partial(6)
    beside_down(1)
    z_sum(2)
    opposite(2)
    partial(7)
    own_half.wait()
    project((0, 0), 0)
    project_y((0, 0))
    project((0, 1), 0)
    weight_z(3)
    project((3, 0), 0)
    project((1, 0), 0)
    weight_opposite()
    z_sum(1)
    beside_up(2)
    project((3, 1), 0)
    project((2, 0), 0)
    pass_on(1)
    weight_z(1)
    project((1, 1), 0)
    finish_across()
    z_sum(3)
    beside_down(2)
    project_y((3, 0))
    project_y((1, 0))
    weight_z(2)
    project((2, 1), 0)
    pass_on(2)
    project_y((0, 1))
    project_y((2, 0))
    finish_here()
    p_local = exact(q_ref[:, 0:512], merged[:, 0:512], ((1,), (1,)))
    finish_second()
    p_local = p_local + exact(q_ref[:, 512:1024], merged[:, 512:1024], ((1,), (1,)))
    pa_slots[y] = p_local.astype(BF16)
    spread(go, "pa", lambda k: pa_slots.at[y], pa_slots, y, y_of)
    project_y((3, 1))
    project_y((1, 1))
    gathered(go, "pa", y_of)
    pb_slots[zh] = total_of(pa_slots, 4).astype(BF16)
    spread(go, "pb", lambda k: pb_slots.at[zh], pb_slots, zh, z_of)
    project_y((2, 1))
    gathered(go, "pb", z_of)
    factor = total_of(pb_slots, 2) * 0.125

    g_slots[f] = exact(factor, factor, ((1,), (1,)))
    spread(go, "gram", lambda k: g_slots.at[f], g_slots, f, member_of)
    s_local = exact(factor, merged[...], ((1,), (0,))) * 0.125
    for i in range(4):
        for j in range(4):
            s_out[i * 4 + j] = s_local[16 * i : 16 * i + 16, 256 * j : 256 * j + 256]
    spread(go, "s1", lambda k: s_out.at[plane_at[k]], s1, plane, plane_of)
    s1[plane] = s_out[plane]

    gathered(go, "gram", member_of)
    gram = total_of(g_slots, 16)
    row = lax.broadcasted_iota(jnp.int32, (64, 64), 0)
    lane = lax.broadcasted_iota(jnp.int32, (64, 64), 1)
    eye = jnp.where(row == lane, 1.0, 0.0).astype(F32)
    work = jnp.concatenate([eye, gram], axis=1).reshape(8, 8, 128)
    row_id = lax.broadcasted_iota(jnp.int32, (8, 8, 128), 0) * 8 + lax.broadcasted_iota(jnp.int32, (8, 8, 128), 1)

    gathered(go, "s1", plane_of)
    s2[column] = total_of(s1, 16)
    spread(go, "s2", lambda k: s2.at[column], s2, column, column_of)
    for k in range(0, 28, 4):
        work = eliminate(work, k, row_id)

    gathered(go, "s2", column_of)
    s3[plane] = total_of(s2, 8)
    spread(go, "s3", lambda k: s3.at[plane], s3, plane, plane_of)
    for k in range(28, 64, 4):
        work = eliminate(work, k, row_id)
    lane_id = lax.broadcasted_iota(jnp.int32, (8, 8, 128), 2)
    diagonal = jnp.sum(jnp.where(lane_id == row_id + 64, work, 0.0), axis=2, keepdims=True)
    inverse = (work * (1.0 / jnp.sqrt(diagonal))).reshape(64, 128)[:, :64]
    p_hat_ref[...] = jnp.transpose(exact(inverse, factor, ((1,), (0,))))

    for n in range(16):
        go.arrived(("out", n))
        stores[n].wait()
    gathered(go, "s3", plane_of)
    s_total = jnp.concatenate(
        [jnp.concatenate([s3[i * 4 + j] for j in range(4)], axis=1) for i in range(4)], axis=0
    )
    q_next_ref[...] = exact(inverse, s_total, ((1,), (0,)))
    go.finish()


def step(tokens, cotangent, weight, feedback, q_t, grad_scale):
    rows, width = feedback.shape
    rank = q_t.shape[0]
    vmem = pl.BlockSpec(memory_space=pltpu.VMEM)
    hbm = pl.BlockSpec(memory_space=pl.ANY)
    dma = pltpu.SemaphoreType.DMA
    return pl.pallas_call(
        functools.partial(step_kernel, grad_scale),
        out_shape=(
            jax.ShapeDtypeStruct(tokens.shape, BF16),
            jax.ShapeDtypeStruct((rows, width), F32),
            jax.ShapeDtypeStruct((rows, rank), F32),
            jax.ShapeDtypeStruct((rank, width), F32),
        ),
        in_specs=[hbm, hbm, hbm, vmem, vmem],
        out_specs=(hbm, vmem, vmem, vmem),
        scratch_shapes=[
            pltpu.VMEM((8, 1024, 512), BF16),
            pltpu.VMEM((1024, 1024), BF16),
            pltpu.VMEM((8, 512, 1024), BF16),
            pltpu.VMEM((3, 2, 512, 256), BF16),
            pltpu.VMEM((3, 2, 512, 512), BF16),
            pltpu.VMEM((512, 512), BF16),
            pltpu.VMEM((512, 512), BF16),
            pltpu.VMEM((4, 512, 512), BF16),
            pltpu.VMEM((8, 2, 256, 1024), BF16),
            pltpu.VMEM((4, rank, rows), BF16),
            pltpu.VMEM((2, rank, rows), BF16),
            pltpu.VMEM((16, rank, rank), F32),
            pltpu.VMEM((16, 16, 256), F32),
            pltpu.VMEM((16, 16, 256), F32),
            pltpu.VMEM((8, 16, 256), F32),
            pltpu.VMEM((16, 16, 256), F32),
            dma((N_COPIES,)), dma((N_COPIES,)), dma((10,)), dma((16,)),
        ],
        compiler_params=pltpu.CompilerParams(
            collective_id=2, has_side_effects=True, vmem_limit_bytes=60 * 1024 * 1024
        ),
        name="step",
    )(tokens, cotangent, weight, feedback, q_t)


def results_kernel(made, merged, p_hat, q_next, input_grad, feedback_next, q_out, pieces, wide, read_sem, write_sem):
    chunk = pieces.shape[1]
    n = pieces.shape[0]
    first = pltpu.make_async_copy(merged, wide, read_sem.at[n])
    first.start()
    reads, writes = [], []
    for i in range(n):
        rows = pl.ds(i * chunk, chunk)
        reads.append(pltpu.make_async_copy(made.at[rows], pieces.at[i], read_sem.at[i]))
        writes.append(pltpu.make_async_copy(pieces.at[i], input_grad.at[rows], write_sem.at[i]))
        reads[i].start()
    q_out[...] = q_next[...]
    first.wait()
    total = wide.shape[0]
    half = total // 2
    for h in range(2):
        rows = pl.ds(h * half, half)
        wide[rows] = wide[rows] - exact(p_hat[rows], q_next[...], ((1,), (0,)))
        writes.append(pltpu.make_async_copy(wide.at[rows], feedback_next.at[rows], write_sem.at[n + h]))
        writes[n + h].start()
        for i in range(h * n // 2, (h + 1) * n // 2):
            reads[i].wait()
            writes[i].start()
    for write in writes:
        write.wait()


def results(made, merged, p_hat, q_next):
    n = 8
    vmem = pl.BlockSpec(memory_space=pltpu.VMEM)
    hbm = pl.BlockSpec(memory_space=pl.ANY)
    dma = pltpu.SemaphoreType.DMA
    return pl.pallas_call(
        results_kernel,
        out_shape=(
            jax.ShapeDtypeStruct(made.shape, BF16),
            jax.ShapeDtypeStruct(merged.shape, F32),
            jax.ShapeDtypeStruct(q_next.shape, F32),
        ),
        in_specs=[hbm, hbm, vmem, vmem],
        out_specs=(hbm, hbm, vmem),
        scratch_shapes=[
            pltpu.VMEM((n, made.shape[0] // n, made.shape[1]), BF16),
            pltpu.VMEM(merged.shape, F32),
            dma((n + 1,)), dma((n + 2,)),
        ],
        compiler_params=pltpu.CompilerParams(vmem_limit_bytes=24 * 1024 * 1024),
        name="results",
    )(made, merged, p_hat, q_next)


def per_device(tokens, cotangent, weight, feedback, q_factor):
    members = lax.axis_size("fsdp")
    grad_scale = 1.0 / math.sqrt(tokens.shape[0] * members)
    made, merged, p_hat, q_next = step(tokens, cotangent, weight, feedback[0], q_factor.T, grad_scale)
    input_grad, feedback_next, q_next = results(made, merged, p_hat, q_next)
    return (input_grad, q_next.T, feedback_next[None])


def solution(mesh):
    placed = (
        P(("dp", "fsdp"), None),
        P(("dp", "fsdp"), None),
        P("fsdp", None),
        P("dp", "fsdp", None),
        P(),
    )
    return jax.shard_map(
        per_device,
        mesh=mesh,
        in_specs=placed,
        out_specs=(P(("dp", "fsdp"), None), P(), P("dp", "fsdp", None)),
        check_vma=False,
    )
```

```python
import functools
import math

import jax
import jax.numpy as jnp
from jax import lax
from jax.experimental import pallas as pl
from jax.experimental.pallas import tpu as pltpu
from jax.sharding import PartitionSpec as P

MESH = pl.DeviceIdType.MESH
HIGHEST = lax.Precision.HIGHEST
F32 = jnp.float32
BF16 = jnp.bfloat16


def where_am_i():
    d = lax.axis_index("dp")
    f = lax.axis_index("fsdp")
    return d // 4, d % 4, f // 4, (f // 2) % 2, f % 2


def device(zh, y, x, zl, c):
    return (zh * 4 + y, x * 4 + zl * 2 + c)


def exact(left, right, dims):
    return lax.dot_general(left, right, (dims, ((), ())), precision=HIGHEST, preferred_element_type=F32)


def spread(copies, name, src, slots, me, targets):
    for k, target in enumerate(targets):
        copies.start((name, k), src(k), slots.at[me], target)


def gathered(copies, name, targets):
    for k in range(len(targets)):
        copies.arrived((name, k))


def total_of(slots, n):
    total = slots[0].astype(F32)
    for k in range(1, n):
        total = total + slots[k].astype(F32)
    return total


def eliminate(work, k, row_id):
    group, first = k // 8, k % 8
    columns = [jnp.broadcast_to(work[:, :, 64 + k + j : 65 + k + j], (8, 8, 128)) for j in range(4)]
    rows = [jnp.broadcast_to(work[group, first + j : first + j + 1, :], (8, 128)) for j in range(4)]
    pivot = {}
    for j in range(4):
        for i in range(j, 4):
            pivot[i, j] = jnp.broadcast_to(columns[j][group, first + i : first + i + 1, :], (8, 128))
    for j in range(4):
        inverse = 1.0 / pivot[j, j]
        multiplier = columns[j] * inverse
        for i in range(j + 1, 4):
            columns[i] = columns[i] - multiplier * pivot[i, j]
            scale = pivot[i, j] * inverse
            rows[i] = rows[i] - scale * rows[j]
            for m in range(i, 4):
                pivot[m, i] = pivot[m, i] - scale * pivot[m, j]
        work = work - jnp.where(row_id > k + j, multiplier, 0.0) * rows[j]
    return work


ORDER = [(2, 1), (1, 1), (3, 1), (0, 1), (2, 0), (1, 0), (3, 0), (0, 0)]
SLOT = {relative: o for o, relative in enumerate(ORDER)}
Y_UP = [(0, 0), (3, 0), (2, 0), (1, 1)]
N_COPIES = 160


class Copies:
    def __init__(self, send, recv):
        self.send, self.recv, self.used, self.all = send, recv, 0, {}

    def start(self, name, src, dst, target):
        copy = pltpu.make_async_remote_copy(
            src_ref=src,
            dst_ref=dst,
            send_sem=self.send.at[self.used],
            recv_sem=self.recv.at[self.used],
            device_id=target,
            device_id_type=MESH,
        )
        self.used += 1
        copy.start()
        self.all[name] = copy

    def arrived(self, name):
        self.all[name].wait_recv()

    def finish(self):
        for copy in self.all.values():
            copy.wait_send()


def step_kernel(
    grad_scale, tokens, cotangent, weight, feedback_in, q_in, input_grad, merged, p_hat_ref, q_next_ref,
    tok, cot, part, hop, side, z_last, z_send, z_first, w_all,
    pa_slots, pb_slots, g1_slots, g2_slots, wide_factor, s_out, s1, s2, s3_out, s3, met,
    feedback, q_ref, send, recv, load_sem, store_sem,
):
    zh, y, x, zl, c = where_am_i()
    half = y % 2
    mate = device(zh, y, x, zl, 1 - c)
    x_up, x_down = device(zh, y, (x + 1) % 4, zl, c), device(zh, y, (x + 3) % 4, zl, c)
    y_up, y_down = device(zh, (y + 1) % 4, x, zl, c), device(zh, (y + 3) % 4, x, zl, c)
    z_pair, z_across = device(zh, y, x, 1 - zl, c), device(1 - zh, y, x, 1 - zl, c)
    d = lax.axis_index("dp")
    f = lax.axis_index("fsdp")
    plane = x * 4 + y
    column = zh * 4 + zl * 2 + c
    y_of = [device(zh, (y + k) % 4, x, zl, c) for k in range(1, 4)]
    z_of = [device(1 - zh, y, x, zl, c)]
    group_of = [((d + k) % 8, f) for k in range(1, 8)]
    member_of = [(d, (f + k) % 16) for k in range(1, 16)]
    plane_at = [(plane + k) % 16 for k in range(1, 16)]
    plane_of = [device(zh, t % 4, t // 4, zl, c) for t in plane_at]
    column_at = [(column + k) % 8 for k in range(1, 8)]
    column_of = [device(t // 4, y, x, (t // 2) % 2, t % 2) for t in column_at]
    partners = [mate, x_up, x_down, y_up, y_down, z_pair, z_across]

    def first_row(relative, core):
        rx, rz = relative
        return (((x + rx) % 4) * 4 + ((zl + rz) % 2) * 2 + core) * 512

    barrier = pltpu.get_barrier_semaphore()
    for target in partners:
        pl.semaphore_signal(barrier, inc=1, device_id=target, device_id_type=MESH)
    loads = [pltpu.make_async_copy(cotangent, cot.at[0:512], load_sem.at[8])]
    for o, relative in enumerate(ORDER):
        columns = pl.ds(pl.multiple_of(first_row(relative, c), 512), 512)
        loads.append(pltpu.make_async_copy(tokens.at[:, columns], tok.at[o, 0:512], load_sem.at[o]))
    late = [
        pltpu.make_async_copy(feedback_in, feedback, load_sem.at[10]),
        pltpu.make_async_copy(q_in, q_ref, load_sem.at[11]),
    ]
    for load in loads + late:
        load.start()
    pl.semaphore_wait(barrier, len(partners))

    rounds = [[x_up, x_down], [y_up, y_down], [y_up, y_down], [z_pair, z_across], [z_pair, z_across], [mate]]

    def meet(n):
        if n > 0:
            pl.semaphore_wait(met.at[n - 1], len(rounds[n - 1]))
        if n < len(rounds):
            for target in rounds[n]:
                pl.semaphore_signal(met.at[n], inc=1, device_id=target, device_id_type=MESH)

    go = Copies(send, recv)
    go.start("cot", cotangent, cot.at[512:1024], mate)
    for o, relative in enumerate(ORDER):
        columns = pl.ds(pl.multiple_of(first_row(relative, 1 - c), 512), 512)
        go.start(("tok", o), tokens.at[:, columns], tok.at[o, 512:1024], mate)

    my_half = weight.at[pl.ds(pl.multiple_of(half * 256, 256), 256)]
    own_half = pltpu.make_async_copy(my_half, w_all.at[SLOT[0, 0], 0], load_sem.at[9])
    own_half.start()
    go.start(("wx", 3), my_half, w_all.at[SLOT[3, 0], 0], x_up)
    go.start(("wx", 1), my_half, w_all.at[SLOT[1, 0], 0], x_down)
    go.start(("wz", 0), my_half, w_all.at[SLOT[0, 1], 0], z_across)
    go.start(("wy", (0, 0)), my_half, w_all.at[SLOT[0, 0], 1], y_up)

    def weight_y(relative):
        target = y_up if relative in Y_UP else y_down
        go.start(("wy", relative), w_all.at[SLOT[relative], 0], w_all.at[SLOT[relative], 1], target)

    def weight_x():
        go.arrived(("wx", 3))
        go.start(("wf", 0), w_all.at[SLOT[3, 0], 0, 0:128], w_all.at[SLOT[2, 0], 0, 0:128], x_up)
        go.start(("wz", 3), w_all.at[SLOT[3, 0], 0], w_all.at[SLOT[3, 1], 0], z_across)
        weight_y((3, 0))
        go.arrived(("wx", 1))
        go.start(("wf", 1), w_all.at[SLOT[1, 0], 0, 128:256], w_all.at[SLOT[2, 0], 0, 128:256], x_down)
        go.start(("wz", 1), w_all.at[SLOT[1, 0], 0], w_all.at[SLOT[1, 1], 0], z_across)
        weight_y((1, 0))

    def weight_opposite():
        go.arrived(("wf", 0))
        go.arrived(("wf", 1))
        go.start(("wz", 2), w_all.at[SLOT[2, 0], 0], w_all.at[SLOT[2, 1], 0], z_across)
        weight_y((2, 0))

    def weight_z(rx):
        go.arrived(("wz", rx))
        weight_y((rx, 1))

    stores = []

    def project(relative, which):
        n = len(stores)
        slot = SLOT[relative]

        @pl.loop(0, 4)
        def _(i):
            rows = pl.ds(pl.multiple_of(i * 256, 256), 256)
            tok[slot, rows, 256 * which : 256 * which + 256] = lax.dot_general(
                cot[rows], w_all[slot, which], (((1,), (1,)), ((), ())), preferred_element_type=F32
            ).astype(BF16)

        column = first_row(relative, c) + (half if which == 0 else 1 - half) * 256
        columns = pl.ds(pl.multiple_of(column, 256), 256)
        made = tok.at[slot, :, 256 * which : 256 * which + 256]
        store = pltpu.make_async_copy(made.at[0:512], input_grad.at[:, columns], store_sem.at[n])
        store.start()
        stores.append(store)
        go.start(("out", n), made.at[512:1024], input_grad.at[:, columns], mate)

    def project_y(relative):
        go.arrived(("wy", relative))
        project(relative, 1)

    def partial(o):
        loads[1 + o].wait()
        go.arrived(("tok", o))

        @pl.loop(0, 2)
        def _(i):
            rows = pl.ds(pl.multiple_of(i * 256, 256), 256)
            part[o, rows] = lax.dot_general(
                tok[o, :, rows], cot[...], (((0,), (0,)), ((), ())), preferred_element_type=F32
            ).astype(BF16)

    START = [0, 0, 512]
    ACROSS = [1, 0, 0]

    def columns_of(s, which):
        return pl.ds(START[s] + 256 * which, 256)

    def opposite(s):
        src = part.at[SLOT[2, ACROSS[s]]]
        go.start(("hop", s, 0), src.at[:, columns_of(s, 0)], hop.at[s, 0], x_up)
        go.start(("hop", s, 1), src.at[:, columns_of(s, 1)], hop.at[s, 1], x_down)

    def beside_up(s):
        src = part.at[SLOT[1, ACROSS[s]]]
        go.start(("side", s, 0, 1), src.at[:, columns_of(s, 1)], side.at[s, 0, :, 256:512], x_up)

    def beside_down(s):
        src = part.at[SLOT[3, ACROSS[s]]]
        go.start(("side", s, 1, 0), src.at[:, columns_of(s, 0)], side.at[s, 1, :, 0:256], x_down)

    def add_into(dst, dst_columns, src, src_columns):
        @pl.loop(0, 4)
        def _(i):
            rows = pl.ds(pl.multiple_of(i * 128, 128), 128)
            dst[rows, dst_columns] = (
                dst[rows, dst_columns].astype(F32) + src[rows, src_columns].astype(F32)
            ).astype(BF16)

    def pass_on(s):
        for which, rx, target in ((0, 1, x_up), (1, 3, x_down)):
            go.arrived(("hop", s, which))
            mine = part.at[SLOT[rx, ACROSS[s]]]
            add_into(mine, columns_of(s, which), hop.at[s, which], pl.ds(0, 256))
            for r in range(2 if s == 2 else 1):
                rows = pl.ds(256 * r, 256) if s == 2 else pl.ds(0, 512)
                go.start(
                    ("side", s, which, which) if s < 2 else ("last", which, r), mine.at[rows, columns_of(s, which)],
                    side.at[s, which, rows, 256 * which : 256 * which + 256], target,
                )

    def sides_arrived(s):
        for which in range(2):
            for columns in range(2):
                go.arrived(("side", s, which, columns))

    def z_exchange(rx):
        go.start(("z1", rx), part.at[SLOT[rx, 1], :, 512:1024], z_first.at[rx], z_pair)

    def z_sum(rx):
        go.arrived(("z1", rx))
        add_into(part.at[SLOT[rx, 0]], pl.ds(512, 512), z_first.at[rx], pl.ds(0, 512))

    def finish_across():
        sides_arrived(0)

        @pl.loop(0, 4)
        def _(i):
            rows = pl.ds(pl.multiple_of(i * 128, 128), 128)
            z_send[rows] = (
                part[SLOT[0, 1], rows, 0:512].astype(F32)
                + side[0, 0, rows].astype(F32)
                + side[0, 1, rows].astype(F32)
            ).astype(BF16)

        go.start("z2", z_send, z_last, z_pair)

    def finish_here():
        sides_arrived(1)
        go.arrived("z2")

        @pl.loop(0, 4)
        def _(i):
            rows = pl.ds(pl.multiple_of(i * 128, 128), 128)
            total = (
                part[SLOT[0, 0], rows, 0:512].astype(F32)
                + side[1, 0, rows].astype(F32)
                + side[1, 1, rows].astype(F32)
                + z_last[rows].astype(F32)
            )
            merged[rows, 0:512] = feedback[rows, 0:512] + total * grad_scale

    def finish_second(r):
        if r == 0:
            go.arrived(("side", 2, 0, 1))
            go.arrived(("side", 2, 1, 0))
            go.arrived(("z1", 0))
        for which in range(2):
            go.arrived(("last", which, r))

        @pl.loop(2 * r, 2 * r + 2)
        def _(i):
            rows = pl.ds(pl.multiple_of(i * 128, 128), 128)
            total = (
                part[SLOT[0, 0], rows, 512:1024].astype(F32)
                + side[2, 0, rows].astype(F32)
                + side[2, 1, rows].astype(F32)
                + z_first[0, rows].astype(F32)
            )
            merged[rows, 512:1024] = feedback[rows, 512:1024] + total * grad_scale

    loads[0].wait()
    go.arrived("cot")
    partial(0)
    meet(0)
    opposite(0)
    z_exchange(2)
    partial(1)
    meet(1)
    beside_up(0)
    z_exchange(1)
    partial(2)
    meet(2)
    beside_down(0)
    z_exchange(3)
    partial(3)
    meet(3)
    z_exchange(0)
    weight_x()
    partial(4)
    meet(4)
    opposite(1)
    weight_z(0)
    partial(5)
    meet(5)
    beside_up(1)
    pass_on(0)
    partial(6)
    meet(6)
    beside_down(1)
    z_sum(2)
    opposite(2)
    partial(7)
    own_half.wait()
    for load in late:
        load.wait()
    project((0, 0), 0)
    project_y((0, 0))
    project((0, 1), 0)
    weight_z(3)
    project((3, 0), 0)
    project((1, 0), 0)
    weight_opposite()
    z_sum(1)
    beside_up(2)
    project((3, 1), 0)
    project((2, 0), 0)
    pass_on(1)
    weight_z(1)
    project((1, 1), 0)
    finish_across()
    z_sum(3)
    beside_down(2)
    project_y((3, 0))
    project_y((1, 0))
    weight_z(2)
    project((2, 1), 0)
    pass_on(2)
    project_y((0, 1))
    project_y((2, 0))
    finish_here()
    p_first = exact(q_ref[:, 0:512], merged[:, 0:512], ((1,), (1,)))
    for r in range(2):
        finish_second(r)
        rows = slice(256 * r, 256 * r + 256)
        p_local = p_first[:, rows] + exact(q_ref[:, 512:1024], merged[rows, 512:1024], ((1,), (1,)))
        pa_slots[r, y] = p_local.astype(BF16)
        spread(go, ("pa", r), lambda k: pa_slots.at[r, y], pa_slots.at[r], y, y_of)
    project_y((3, 1))
    for r in range(2):
        gathered(go, ("pa", r), y_of)
        pb_slots[r, zh] = total_of(pa_slots.at[r], 4).astype(BF16)
        spread(go, ("pb", r), lambda k: pb_slots.at[r, zh], pb_slots.at[r], zh, z_of)
    project_y((1, 1))
    s_local = None
    for r in range(2):
        gathered(go, ("pb", r), z_of)
        rows = slice(256 * r, 256 * r + 256)
        factor = total_of(pb_slots.at[r], 2) * 0.125
        wide_factor[:, rows] = factor
        s_part = exact(factor, merged[rows], ((1,), (0,)))
        s_local = s_part if s_local is None else s_local + s_part
    for i in range(4):
        for j in range(4):
            s_out[i * 4 + j] = (s_local[16 * i : 16 * i + 16, 256 * j : 256 * j + 256] * 0.125).astype(BF16)
    spread(go, "s1", lambda k: s_out.at[plane_at[k]], s1, plane, plane_of)
    mine = wide_factor[pl.ds(pl.multiple_of(d * 8, 8), 8)]
    factor = wide_factor[...]
    g1_slots[f] = exact(mine, factor, ((1,), (1,)))
    spread(go, "g1", lambda k: g1_slots.at[f], g1_slots, f, member_of)
    s1[plane] = s_out[plane]
    project_y((2, 1))
    gathered(go, "g1", member_of)
    g2_slots[d] = total_of(g1_slots, 16)
    spread(go, "g2", lambda k: g2_slots.at[d], g2_slots, d, group_of)

    gathered(go, "s1", plane_of)
    s2[column] = total_of(s1, 16)
    spread(go, "s2", lambda k: s2.at[column], s2, column, column_of)
    gathered(go, "g2", group_of)
    group = lax.broadcasted_iota(jnp.int32, (8, 8, 64), 0)
    row = lax.broadcasted_iota(jnp.int32, (8, 8, 64), 1)
    lane = lax.broadcasted_iota(jnp.int32, (8, 8, 64), 2)
    eye = jnp.where(group * 8 + row == lane, 1.0, 0.0).astype(F32)
    work = jnp.concatenate([eye, g2_slots[...]], axis=2)
    row_id = lax.broadcasted_iota(jnp.int32, (8, 8, 128), 0) * 8 + lax.broadcasted_iota(jnp.int32, (8, 8, 128), 1)
    for k in range(0, 16, 4):
        work = eliminate(work, k, row_id)

    gathered(go, "s2", column_of)
    s3_out[...] = total_of(s2, 8).astype(BF16)
    s3[plane] = s3_out[...]
    spread(go, "s3", lambda k: s3_out, s3, plane, plane_of)
    for k in range(16, 64, 4):
        work = eliminate(work, k, row_id)
    lane_id = lax.broadcasted_iota(jnp.int32, (8, 8, 128), 2)
    diagonal = jnp.sum(jnp.where(lane_id == row_id + 64, work, 0.0), axis=2, keepdims=True)
    inverse = (work * (1.0 / jnp.sqrt(diagonal))).reshape(64, 128)[:, :64]
    p_hat_ref[...] = jnp.transpose(exact(inverse, factor, ((1,), (0,))))

    for n in range(16):
        go.arrived(("out", n))
        stores[n].wait()
    gathered(go, "s3", plane_of)
    s_total = jnp.concatenate(
        [jnp.concatenate([s3[i * 4 + j] for j in range(4)], axis=1) for i in range(4)], axis=0
    ).astype(F32)
    q_next_ref[...] = exact(inverse, s_total, ((1,), (0,)))
    go.finish()


def step(tokens, cotangent, weight, feedback, q_t, grad_scale):
    rows, width = feedback.shape
    rank = q_t.shape[0]
    vmem = pl.BlockSpec(memory_space=pltpu.VMEM)
    hbm = pl.BlockSpec(memory_space=pltpu.HBM)
    dma = pltpu.SemaphoreType.DMA
    return pl.pallas_call(
        functools.partial(step_kernel, grad_scale),
        out_shape=(
            pltpu.VMEM(tokens.shape, BF16),
            pltpu.VMEM((rows, width), F32),
            pltpu.VMEM((rows, rank), F32),
            pltpu.VMEM((rank, width), F32),
        ),
        in_specs=[hbm] * 5,
        out_specs=(vmem,) * 4,
        scratch_shapes=[
            pltpu.VMEM((8, 1024, 512), BF16),
            pltpu.VMEM((1024, 1024), BF16),
            pltpu.VMEM((8, 512, 1024), BF16),
            pltpu.VMEM((3, 2, 512, 256), BF16),
            pltpu.VMEM((3, 2, 512, 512), BF16),
            pltpu.VMEM((512, 512), BF16),
            pltpu.VMEM((512, 512), BF16),
            pltpu.VMEM((4, 512, 512), BF16),
            pltpu.VMEM((8, 2, 256, 1024), BF16),
            pltpu.VMEM((2, 4, rank, rows // 2), BF16),
            pltpu.VMEM((2, 2, rank, rows // 2), BF16),
            pltpu.VMEM((16, 8, rank), F32),
            pltpu.VMEM((8, 8, rank), F32),
            pltpu.VMEM((rank, rows), F32),
            pltpu.VMEM((16, 16, 256), BF16),
            pltpu.VMEM((16, 16, 256), BF16),
            pltpu.VMEM((8, 16, 256), F32),
            pltpu.VMEM((16, 256), BF16),
            pltpu.VMEM((16, 16, 256), BF16),
            pltpu.SemaphoreType.REGULAR((6,)),
            pltpu.VMEM((rows, width), F32),
            pltpu.VMEM((rank, width), F32),
            dma((N_COPIES,)), dma((N_COPIES,)), dma((12,)), dma((16,)),
        ],
        compiler_params=pltpu.CompilerParams(
            collective_id=2, has_side_effects=True, vmem_limit_bytes=50 * 1024 * 1024
        ),
        name="step",
    )(tokens, cotangent, weight, feedback, q_t)


def results_kernel(made, merged, p_hat, q_next, input_grad, feedback_next, q_out, wide, write_sem):
    writes = [
        pltpu.make_async_copy(made, input_grad, write_sem.at[0]),
        pltpu.make_async_copy(q_next, q_out, write_sem.at[1]),
    ]
    for write in writes:
        write.start()
    half = wide.shape[0] // 2
    for h in range(2):
        rows = pl.ds(h * half, half)
        wide[rows] = merged[rows] - exact(p_hat[rows], q_next[...], ((1,), (0,)))
        writes.append(pltpu.make_async_copy(wide.at[rows], feedback_next.at[rows], write_sem.at[2 + h]))
        writes[2 + h].start()
    for write in writes:
        write.wait()


def results(made, merged, p_hat, q_next):
    vmem = pl.BlockSpec(memory_space=pltpu.VMEM)
    hbm = pl.BlockSpec(memory_space=pltpu.HBM)
    return pl.pallas_call(
        results_kernel,
        out_shape=(
            jax.ShapeDtypeStruct(made.shape, BF16),
            jax.ShapeDtypeStruct(merged.shape, F32),
            jax.ShapeDtypeStruct(q_next.shape, F32),
        ),
        in_specs=[vmem] * 4,
        out_specs=(hbm,) * 3,
        scratch_shapes=[pltpu.VMEM(merged.shape, F32), pltpu.SemaphoreType.DMA((4,))],
        compiler_params=pltpu.CompilerParams(vmem_limit_bytes=16 * 1024 * 1024),
        name="results",
    )(made, merged, p_hat, q_next)


def per_device(tokens, cotangent, weight, feedback, q_factor):
    members = lax.axis_size("fsdp")
    grad_scale = 1.0 / math.sqrt(tokens.shape[0] * members)
    made, merged, p_hat, q_next = step(tokens, cotangent, weight, feedback[0], q_factor.T, grad_scale)
    input_grad, feedback_next, q_next = results(made, merged, p_hat, q_next)
    return (input_grad, q_next.T, feedback_next[None])


def solution(mesh):
    placed = (
        P(("dp", "fsdp"), None),
        P(("dp", "fsdp"), None),
        P("fsdp", None),
        P("dp", "fsdp", None),
        P(),
    )
    return jax.shard_map(
        per_device,
        mesh=mesh,
        in_specs=placed,
        out_specs=(P(("dp", "fsdp"), None), P(), P("dp", "fsdp", None)),
        check_vma=False,
    )
```

```python
import functools
import math

import jax
import jax.numpy as jnp
from jax import lax
from jax.experimental import pallas as pl
from jax.experimental.pallas import tpu as pltpu
from jax.sharding import PartitionSpec as P

MESH = pl.DeviceIdType.MESH
HIGHEST = lax.Precision.HIGHEST
F32 = jnp.float32
BF16 = jnp.bfloat16


def where_am_i():
    d = lax.axis_index("dp")
    f = lax.axis_index("fsdp")
    return d // 4, d % 4, f // 4, (f // 2) % 2, f % 2


def device(zh, y, x, zl, c):
    return (zh * 4 + y, x * 4 + zl * 2 + c)


def exact(left, right, dims):
    return lax.dot_general(left, right, (dims, ((), ())), precision=HIGHEST, preferred_element_type=F32)


def spread(copies, name, src, slots, me, targets):
    for k, target in enumerate(targets):
        copies.start((name, k), src(k), slots.at[me], target)


def gathered(copies, name, targets):
    for k in range(len(targets)):
        copies.arrived((name, k))


def total_of(slots, n):
    total = slots[0].astype(F32)
    for k in range(1, n):
        total = total + slots[k].astype(F32)
    return total


def eliminate(work, k, row_id):
    group, first = k // 8, k % 8
    columns = [jnp.broadcast_to(work[:, :, 64 + k + j : 65 + k + j], (8, 8, 128)) for j in range(4)]
    rows = [jnp.broadcast_to(work[group, first + j : first + j + 1, :], (8, 128)) for j in range(4)]
    pivot = {}
    for j in range(4):
        for i in range(j, 4):
            pivot[i, j] = jnp.broadcast_to(columns[j][group, first + i : first + i + 1, :], (8, 128))
    for j in range(4):
        inverse = 1.0 / pivot[j, j]
        multiplier = columns[j] * inverse
        for i in range(j + 1, 4):
            columns[i] = columns[i] - multiplier * pivot[i, j]
            scale = pivot[i, j] * inverse
            rows[i] = rows[i] - scale * rows[j]
            for m in range(i, 4):
                pivot[m, i] = pivot[m, i] - scale * pivot[m, j]
        work = work - jnp.where(row_id > k + j, multiplier, 0.0) * rows[j]
    return work


ORDER = [(2, 1), (1, 1), (3, 1), (0, 1), (2, 0), (1, 0), (3, 0), (0, 0)]
SLOT = {relative: o for o, relative in enumerate(ORDER)}
N_COPIES = 160


class Copies:
    def __init__(self, send, recv):
        self.send, self.recv, self.used, self.all = send, recv, 0, {}

    def start(self, name, src, dst, target):
        copy = pltpu.make_async_remote_copy(
            src_ref=src,
            dst_ref=dst,
            send_sem=self.send.at[self.used],
            recv_sem=self.recv.at[self.used],
            device_id=target,
            device_id_type=MESH,
        )
        self.used += 1
        copy.start()
        self.all[name] = copy

    def arrived(self, name):
        self.all[name].wait_recv()

    def finish(self):
        for copy in self.all.values():
            copy.wait_send()


def step_kernel(
    grad_scale, tokens, cotangent, weight, feedback_in, q_in, input_grad, merged, p_hat_ref, q_next_ref,
    tok, cot, part, hop, side, z_last, z_send, z_first, w_all,
    pa_slots, pb_slots, g1_slots, g2_slots, wide_factor, s_out, s1, s2, s3_out, s3, met,
    feedback, q_ref, send, recv, load_sem, store_sem,
):
    zh, y, x, zl, c = where_am_i()
    mate = device(zh, y, x, zl, 1 - c)
    x_up, x_down = device(zh, y, (x + 1) % 4, zl, c), device(zh, y, (x + 3) % 4, zl, c)
    y_up, y_down = device(zh, (y + 1) % 4, x, zl, c), device(zh, (y + 3) % 4, x, zl, c)
    z_pair, z_across = device(zh, y, x, 1 - zl, c), device(1 - zh, y, x, 1 - zl, c)
    d = lax.axis_index("dp")
    f = lax.axis_index("fsdp")
    plane = x * 4 + y
    column = zh * 4 + zl * 2 + c
    y_of = [device(zh, (y + k) % 4, x, zl, c) for k in range(1, 4)]
    z_of = [device(1 - zh, y, x, zl, c)]
    group_of = [((d + k) % 8, f) for k in range(1, 8)]
    member_of = [(d, (f + k) % 16) for k in range(1, 16)]
    plane_at = [(plane + k) % 16 for k in range(1, 16)]
    plane_of = [device(zh, t % 4, t // 4, zl, c) for t in plane_at]
    column_at = [(column + k) % 8 for k in range(1, 8)]
    column_of = [device(t // 4, y, x, (t // 2) % 2, t % 2) for t in column_at]
    partners = [mate, x_up, x_down, y_up, y_down, z_pair, z_across]

    def first_row(relative, core):
        rx, rz = relative
        return (((x + rx) % 4) * 4 + ((zl + rz) % 2) * 2 + core) * 512

    barrier = pltpu.get_barrier_semaphore()
    for target in partners:
        pl.semaphore_signal(barrier, inc=1, device_id=target, device_id_type=MESH)
    loads = [pltpu.make_async_copy(cotangent, cot.at[0:512], load_sem.at[8])]
    for o, relative in enumerate(ORDER):
        columns = pl.ds(pl.multiple_of(first_row(relative, c), 512), 512)
        loads.append(pltpu.make_async_copy(tokens.at[:, columns], tok.at[o, 0:512], load_sem.at[o]))
    late = [
        pltpu.make_async_copy(feedback_in, feedback, load_sem.at[10]),
        pltpu.make_async_copy(q_in, q_ref, load_sem.at[11]),
    ]
    for load in loads + late:
        load.start()
    pl.semaphore_wait(barrier, len(partners))

    rounds = [[x_up, x_down], [y_up, y_down], [y_up, y_down], [z_pair, z_across], [z_pair, z_across], [mate]]

    def meet(n):
        if n > 0:
            pl.semaphore_wait(met.at[n - 1], len(rounds[n - 1]))
        if n < len(rounds):
            for target in rounds[n]:
                pl.semaphore_signal(met.at[n], inc=1, device_id=target, device_id_type=MESH)

    go = Copies(send, recv)
    go.start(("cot", 1), cotangent.at[:, 512:1024], cot.at[512:1024, 512:1024], mate)
    for o, relative in enumerate(ORDER):
        columns = pl.ds(pl.multiple_of(first_row(relative, 1 - c), 512), 512)
        go.start(("tok", o), tokens.at[:, columns], tok.at[o, 512:1024], mate)
        if o == 0:
            go.start(("cot", 0), cotangent.at[:, 0:512], cot.at[512:1024, 0:512], mate)

    def quarter(of, start=0, size=128):
        return pl.ds(pl.multiple_of(of * 128 + start, 64), size)

    mine = quarter(y)
    below, above = (y + 3) % 4, (y + 1) % 4
    own_shard = pltpu.make_async_copy(weight, w_all.at[SLOT[0, 0]], load_sem.at[9])
    own_shard.start()
    go.start(("wx", 3), weight.at[mine], w_all.at[SLOT[3, 0], mine], x_up)
    go.start(("wx", 1), weight.at[mine], w_all.at[SLOT[1, 0], mine], x_down)
    go.start(("w0", 0), weight.at[0:256], w_all.at[SLOT[0, 1], 0:256], z_across)

    def same(name, relative, rows, target):
        src = w_all.at[SLOT[relative], rows]
        go.start((name, relative), src, src, target)

    def weight_y(relative):
        same("yu", relative, mine, y_up)
        same("yd", relative, mine, y_down)

    def forward_y(relative):
        go.arrived(("yu", relative))
        same("fu", relative, quarter(below, 0, 64), y_up)
        go.arrived(("yd", relative))
        same("fd", relative, quarter(above, 64, 64), y_down)

    def weight_x():
        for rx, start, target in ((3, 0, x_up), (1, 64, x_down)):
            go.arrived(("wx", rx))
            rows = quarter(y, start, 64)
            go.start(("wf", rx), w_all.at[SLOT[rx, 0], rows], w_all.at[SLOT[2, 0], rows], target)
            go.start(("wz", rx), w_all.at[SLOT[rx, 0], mine], w_all.at[SLOT[rx, 1], mine], z_across)
            weight_y((rx, 0))

    def weight_opposite():
        go.arrived(("wf", 3))
        go.arrived(("wf", 1))
        go.start(("wz", 2), w_all.at[SLOT[2, 0], mine], w_all.at[SLOT[2, 1], mine], z_across)
        go.start(("w0", 1), weight.at[256:512], w_all.at[SLOT[0, 1], 256:512], z_across)
        weight_y((2, 0))

    def weight_z(rx):
        go.arrived(("wz", rx))
        weight_y((rx, 1))

    stores = []

    def project(relative):
        n = len(stores)
        slot = SLOT[relative]
        if relative == (0, 0):
            own_shard.wait()
        elif relative == (0, 1):
            go.arrived(("w0", 0))
            go.arrived(("w0", 1))
        else:
            go.arrived(("fu", relative))
            go.arrived(("fd", relative))

        @pl.loop(0, 4)
        def _(i):
            rows = pl.ds(pl.multiple_of(i * 256, 256), 256)
            tok[slot, rows] = lax.dot_general(
                cot[rows], w_all[slot], (((1,), (1,)), ((), ())), preferred_element_type=F32
            ).astype(BF16)

        columns = pl.ds(pl.multiple_of(first_row(relative, c), 512), 512)
        made = tok.at[slot]
        store = pltpu.make_async_copy(made.at[0:512], input_grad.at[:, columns], store_sem.at[n])
        store.start()
        stores.append(store)
        go.start(("out", n), made.at[512:1024], input_grad.at[:, columns], mate)

    def first_partial(color):
        if color == 1:
            loads[0].wait()
            loads[1].wait()
            go.arrived(("tok", 0))
        go.arrived(("cot", color))
        columns = slice(512 * color, 512 * color + 512)

        @pl.loop(0, 2)
        def _(i):
            rows = pl.ds(pl.multiple_of(i * 256, 256), 256)
            part[0, rows, columns] = lax.dot_general(
                tok[0, :, rows], cot[:, columns], (((0,), (0,)), ((), ())), preferred_element_type=F32
            ).astype(BF16)

    def partial(o):
        loads[1 + o].wait()
        go.arrived(("tok", o))

        @pl.loop(0, 2)
        def _(i):
            rows = pl.ds(pl.multiple_of(i * 256, 256), 256)
            part[o, rows] = lax.dot_general(
                tok[o, :, rows], cot[...], (((0,), (0,)), ((), ())), preferred_element_type=F32
            ).astype(BF16)

    START = [0, 0, 512]
    ACROSS = [1, 0, 0]

    def columns_of(s, which):
        return pl.ds(START[s] + 256 * which, 256)

    def opposite(s):
        src = part.at[SLOT[2, ACROSS[s]]]
        go.start(("hop", s, 0), src.at[:, columns_of(s, 0)], hop.at[s, 0], x_up)
        go.start(("hop", s, 1), src.at[:, columns_of(s, 1)], hop.at[s, 1], x_down)

    def beside_up(s):
        src = part.at[SLOT[1, ACROSS[s]]]
        go.start(("side", s, 0, 1), src.at[:, columns_of(s, 1)], side.at[s, 0, :, 256:512], x_up)

    def beside_down(s):
        src = part.at[SLOT[3, ACROSS[s]]]
        go.start(("side", s, 1, 0), src.at[:, columns_of(s, 0)], side.at[s, 1, :, 0:256], x_down)

    def add_into(dst, dst_columns, src, src_columns):
        @pl.loop(0, 4)
        def _(i):
            rows = pl.ds(pl.multiple_of(i * 128, 128), 128)
            dst[rows, dst_columns] = (
                dst[rows, dst_columns].astype(F32) + src[rows, src_columns].astype(F32)
            ).astype(BF16)

    def pass_on(s):
        for which, rx, target in ((0, 1, x_up), (1, 3, x_down)):
            go.arrived(("hop", s, which))
            mine = part.at[SLOT[rx, ACROSS[s]]]
            add_into(mine, columns_of(s, which), hop.at[s, which], pl.ds(0, 256))
            for r in range(2 if s == 2 else 1):
                rows = pl.ds(256 * r, 256) if s == 2 else pl.ds(0, 512)
                go.start(
                    ("side", s, which, which) if s < 2 else ("last", which, r), mine.at[rows, columns_of(s, which)],
                    side.at[s, which, rows, 256 * which : 256 * which + 256], target,
                )

    def sides_arrived(s):
        for which in range(2):
            for columns in range(2):
                go.arrived(("side", s, which, columns))

    def z_exchange(rx):
        go.start(("z1", rx), part.at[SLOT[rx, 1], :, 512:1024], z_first.at[rx], z_pair)

    def z_sum(rx):
        go.arrived(("z1", rx))
        add_into(part.at[SLOT[rx, 0]], pl.ds(512, 512), z_first.at[rx], pl.ds(0, 512))

    def finish_across():
        sides_arrived(0)

        @pl.loop(0, 4)
        def _(i):
            rows = pl.ds(pl.multiple_of(i * 128, 128), 128)
            z_send[rows] = (
                part[SLOT[0, 1], rows, 0:512].astype(F32)
                + side[0, 0, rows].astype(F32)
                + side[0, 1, rows].astype(F32)
            ).astype(BF16)

        for r in range(2):
            rows = pl.ds(256 * r, 256)
            go.start(("z2", r), z_send.at[rows], z_last.at[rows], z_pair)

    def finish_here(r):
        if r == 0:
            sides_arrived(1)
        go.arrived(("z2", r))

        @pl.loop(2 * r, 2 * r + 2)
        def _(i):
            rows = pl.ds(pl.multiple_of(i * 128, 128), 128)
            total = (
                part[SLOT[0, 0], rows, 0:512].astype(F32)
                + side[1, 0, rows].astype(F32)
                + side[1, 1, rows].astype(F32)
                + z_last[rows].astype(F32)
            )
            merged[rows, 0:512] = feedback[rows, 0:512] + total * grad_scale

    def finish_second(r):
        if r == 0:
            go.arrived(("side", 2, 0, 1))
            go.arrived(("side", 2, 1, 0))
            go.arrived(("z1", 0))
        for which in range(2):
            go.arrived(("last", which, r))

        @pl.loop(2 * r, 2 * r + 2)
        def _(i):
            rows = pl.ds(pl.multiple_of(i * 128, 128), 128)
            total = (
                part[SLOT[0, 0], rows, 512:1024].astype(F32)
                + side[2, 0, rows].astype(F32)
                + side[2, 1, rows].astype(F32)
                + z_first[0, rows].astype(F32)
            )
            merged[rows, 512:1024] = feedback[rows, 512:1024] + total * grad_scale

    first_partial(1)
    z_exchange(2)
    first_partial(0)
    opposite(0)
    meet(0)
    partial(1)
    meet(1)
    beside_up(0)
    z_exchange(1)
    weight_x()
    partial(2)
    meet(2)
    beside_down(0)
    z_exchange(3)
    partial(3)
    meet(3)
    z_exchange(0)
    partial(4)
    meet(4)
    opposite(1)
    partial(5)
    meet(5)
    beside_up(1)
    pass_on(0)
    forward_y((3, 0))
    partial(6)
    meet(6)
    beside_down(1)
    z_sum(2)
    opposite(2)
    weight_opposite()
    partial(7)
    forward_y((1, 0))
    weight_z(3)
    weight_z(1)
    for load in late:
        load.wait()
    project((0, 0))
    z_sum(1)
    beside_up(2)
    weight_z(2)
    pass_on(1)
    project((3, 0))
    forward_y((2, 0))
    project((1, 0))
    finish_across()
    z_sum(3)
    beside_down(2)
    forward_y((3, 1))
    project((0, 1))
    forward_y((1, 1))
    pass_on(2)
    forward_y((2, 1))
    project((2, 0))
    project((3, 1))
    for r in range(2):
        finish_here(r)
        finish_second(r)
        rows = slice(256 * r, 256 * r + 256)
        p_local = exact(q_ref[...], merged[rows], ((1,), (1,)))
        pa_slots[r, y] = p_local.astype(BF16)
        spread(go, ("pa", r), lambda k: pa_slots.at[r, y], pa_slots.at[r], y, y_of)
    project((1, 1))
    for r in range(2):
        gathered(go, ("pa", r), y_of)
        pb_slots[r, zh] = total_of(pa_slots.at[r], 4).astype(BF16)
        spread(go, ("pb", r), lambda k: pb_slots.at[r, zh], pb_slots.at[r], zh, z_of)
    s_local = None
    for r in range(2):
        gathered(go, ("pb", r), z_of)
        rows = slice(256 * r, 256 * r + 256)
        factor = total_of(pb_slots.at[r], 2) * 0.125
        wide_factor[:, rows] = factor
        if r == 1:
            slice_of_p = wide_factor[pl.ds(pl.multiple_of(d * 8, 8), 8)]
            g1_slots[f] = exact(slice_of_p, wide_factor[...], ((1,), (1,)))
            spread(go, "g1", lambda k: g1_slots.at[f], g1_slots, f, member_of)
        s_part = exact(factor, merged[rows], ((1,), (0,)))
        s_local = s_part if s_local is None else s_local + s_part
    factor = wide_factor[...]
    for i in range(4):
        for j in range(4):
            s_out[i * 4 + j] = (s_local[16 * i : 16 * i + 16, 256 * j : 256 * j + 256] * 0.125).astype(BF16)
    spread(go, "s1", lambda k: s_out.at[plane_at[k]], s1, plane, plane_of)
    s1[plane] = s_out[plane]
    project((2, 1))
    gathered(go, "g1", member_of)
    g2_slots[d] = total_of(g1_slots, 16)
    spread(go, "g2", lambda k: g2_slots.at[d], g2_slots, d, group_of)

    gathered(go, "s1", plane_of)
    s2[column] = total_of(s1, 16).astype(BF16)
    spread(go, "s2", lambda k: s2.at[column], s2, column, column_of)
    gathered(go, "g2", group_of)
    group = lax.broadcasted_iota(jnp.int32, (8, 8, 64), 0)
    row = lax.broadcasted_iota(jnp.int32, (8, 8, 64), 1)
    lane = lax.broadcasted_iota(jnp.int32, (8, 8, 64), 2)
    eye = jnp.where(group * 8 + row == lane, 1.0, 0.0).astype(F32)
    work = jnp.concatenate([eye, g2_slots[...]], axis=2)
    row_id = lax.broadcasted_iota(jnp.int32, (8, 8, 128), 0) * 8 + lax.broadcasted_iota(jnp.int32, (8, 8, 128), 1)
    for k in range(0, 16, 4):
        work = eliminate(work, k, row_id)

    gathered(go, "s2", column_of)
    s3_out[...] = total_of(s2, 8).astype(BF16)
    s3[plane] = s3_out[...]
    spread(go, "s3", lambda k: s3_out, s3, plane, plane_of)
    for k in range(16, 64, 4):
        work = eliminate(work, k, row_id)
    lane_id = lax.broadcasted_iota(jnp.int32, (8, 8, 128), 2)
    diagonal = jnp.sum(jnp.where(lane_id == row_id + 64, work, 0.0), axis=2, keepdims=True)
    inverse = (work * (1.0 / jnp.sqrt(diagonal))).reshape(64, 128)[:, :64]
    p_hat_ref[...] = jnp.transpose(exact(inverse, factor, ((1,), (0,))))

    for n in range(8):
        go.arrived(("out", n))
        stores[n].wait()
    gathered(go, "s3", plane_of)
    s_total = jnp.concatenate(
        [jnp.concatenate([s3[i * 4 + j] for j in range(4)], axis=1) for i in range(4)], axis=0
    ).astype(F32)
    q_next_ref[...] = exact(inverse, s_total, ((1,), (0,)))
    go.finish()


def step(tokens, cotangent, weight, feedback, q_t, grad_scale):
    rows, width = feedback.shape
    rank = q_t.shape[0]
    vmem = pl.BlockSpec(memory_space=pltpu.VMEM)
    hbm = pl.BlockSpec(memory_space=pltpu.HBM)
    dma = pltpu.SemaphoreType.DMA
    return pl.pallas_call(
        functools.partial(step_kernel, grad_scale),
        out_shape=(
            pltpu.VMEM(tokens.shape, BF16),
            pltpu.VMEM((rows, width), F32),
            pltpu.VMEM((rows, rank), F32),
            pltpu.VMEM((rank, width), F32),
        ),
        in_specs=[hbm] * 5,
        out_specs=(vmem,) * 4,
        scratch_shapes=[
            pltpu.VMEM((8, 1024, 512), BF16),
            pltpu.VMEM((1024, 1024), BF16),
            pltpu.VMEM((8, 512, 1024), BF16),
            pltpu.VMEM((3, 2, 512, 256), BF16),
            pltpu.VMEM((3, 2, 512, 512), BF16),
            pltpu.VMEM((512, 512), BF16),
            pltpu.VMEM((512, 512), BF16),
            pltpu.VMEM((4, 512, 512), BF16),
            pltpu.VMEM((8, 512, 1024), BF16),
            pltpu.VMEM((2, 4, rank, rows // 2), BF16),
            pltpu.VMEM((2, 2, rank, rows // 2), BF16),
            pltpu.VMEM((16, 8, rank), F32),
            pltpu.VMEM((8, 8, rank), F32),
            pltpu.VMEM((rank, rows), F32),
            pltpu.VMEM((16, 16, 256), BF16),
            pltpu.VMEM((16, 16, 256), BF16),
            pltpu.VMEM((8, 16, 256), BF16),
            pltpu.VMEM((16, 256), BF16),
            pltpu.VMEM((16, 16, 256), BF16),
            pltpu.SemaphoreType.REGULAR((6,)),
            pltpu.VMEM((rows, width), F32),
            pltpu.VMEM((rank, width), F32),
            dma((N_COPIES,)), dma((N_COPIES,)), dma((12,)), dma((16,)),
        ],
        compiler_params=pltpu.CompilerParams(
            collective_id=2, has_side_effects=True, vmem_limit_bytes=50 * 1024 * 1024
        ),
        name="step",
    )(tokens, cotangent, weight, feedback, q_t)


def results_kernel(made, merged, p_hat, q_next, input_grad, feedback_next, q_out, wide, write_sem):
    writes = [
        pltpu.make_async_copy(made, input_grad, write_sem.at[0]),
        pltpu.make_async_copy(q_next, q_out, write_sem.at[1]),
    ]
    for write in writes:
        write.start()
    half = wide.shape[0] // 2
    for h in range(2):
        rows = pl.ds(h * half, half)
        wide[rows] = merged[rows] - exact(p_hat[rows], q_next[...], ((1,), (0,)))
        writes.append(pltpu.make_async_copy(wide.at[rows], feedback_next.at[rows], write_sem.at[2 + h]))
        writes[2 + h].start()
    for write in writes:
        write.wait()


def results(made, merged, p_hat, q_next):
    vmem = pl.BlockSpec(memory_space=pltpu.VMEM)
    hbm = pl.BlockSpec(memory_space=pltpu.HBM)
    return pl.pallas_call(
        results_kernel,
        out_shape=(
            jax.ShapeDtypeStruct(made.shape, BF16),
            jax.ShapeDtypeStruct(merged.shape, F32),
            jax.ShapeDtypeStruct(q_next.shape, F32),
        ),
        in_specs=[vmem] * 4,
        out_specs=(hbm,) * 3,
        scratch_shapes=[pltpu.VMEM(merged.shape, F32), pltpu.SemaphoreType.DMA((4,))],
        compiler_params=pltpu.CompilerParams(vmem_limit_bytes=16 * 1024 * 1024),
        name="results",
    )(made, merged, p_hat, q_next)


def per_device(tokens, cotangent, weight, feedback, q_factor):
    members = lax.axis_size("fsdp")
    grad_scale = 1.0 / math.sqrt(tokens.shape[0] * members)
    made, merged, p_hat, q_next = step(tokens, cotangent, weight, feedback[0], q_factor.T, grad_scale)
    input_grad, feedback_next, q_next = results(made, merged, p_hat, q_next)
    return (input_grad, q_next.T, feedback_next[None])


def solution(mesh):
    placed = (
        P(("dp", "fsdp"), None),
        P(("dp", "fsdp"), None),
        P("fsdp", None),
        P("dp", "fsdp", None),
        P(),
    )
    return jax.shard_map(
        per_device,
        mesh=mesh,
        in_specs=placed,
        out_specs=(P(("dp", "fsdp"), None), P(), P("dp", "fsdp", None)),
        check_vma=False,
    )
```

```python
import functools
import math

import jax
import jax.numpy as jnp
from jax import lax
from jax.experimental import pallas as pl
from jax.experimental.pallas import tpu as pltpu
from jax.sharding import PartitionSpec as P

MESH = pl.DeviceIdType.MESH
HIGHEST = lax.Precision.HIGHEST
F32 = jnp.float32
BF16 = jnp.bfloat16


def where_am_i():
    d = lax.axis_index("dp")
    f = lax.axis_index("fsdp")
    return d // 4, d % 4, f // 4, (f // 2) % 2, f % 2


def device(zh, y, x, zl, c):
    return (zh * 4 + y, x * 4 + zl * 2 + c)


def exact(left, right, dims):
    return lax.dot_general(left, right, (dims, ((), ())), precision=HIGHEST, preferred_element_type=F32)


def spread(copies, name, src, slots, me, targets):
    for k, target in enumerate(targets):
        copies.start((name, k), src(k), slots.at[me], target)


def gathered(copies, name, targets):
    for k in range(len(targets)):
        copies.arrived((name, k))


def total_of(slots, n):
    total = slots[0].astype(F32)
    for k in range(1, n):
        total = total + slots[k].astype(F32)
    return total


def eliminate(work, k, row_id):
    group, first = k // 8, k % 8
    done, work, row_id = work[:group], work[group:], row_id[group:]
    columns = [jnp.broadcast_to(work[:, :, 64 + k + j : 65 + k + j], work.shape) for j in range(4)]
    rows = [jnp.broadcast_to(work[0, first + j : first + j + 1, :], (8, 128)) for j in range(4)]
    pivot = {}
    for j in range(4):
        for i in range(j, 4):
            pivot[i, j] = jnp.broadcast_to(columns[j][0, first + i : first + i + 1, :], (8, 128))
    for j in range(4):
        inverse = 1.0 / pivot[j, j]
        multiplier = columns[j] * inverse
        for i in range(j + 1, 4):
            columns[i] = columns[i] - multiplier * pivot[i, j]
            scale = pivot[i, j] * inverse
            rows[i] = rows[i] - scale * rows[j]
            for m in range(i, 4):
                pivot[m, i] = pivot[m, i] - scale * pivot[m, j]
        work = work - jnp.where(row_id > k + j, multiplier, 0.0) * rows[j]
    return work if group == 0 else jnp.concatenate([done, work], axis=0)


ORDER = [(2, 1), (1, 1), (3, 1), (0, 1), (2, 0), (1, 0), (3, 0), (0, 0)]
SLOT = {relative: o for o, relative in enumerate(ORDER)}
N_COPIES = 176
PARTS = 4
ROWS = 512 // PARTS


class Copies:
    def __init__(self, send, recv):
        self.send, self.recv, self.used, self.all = send, recv, 0, {}

    def start(self, name, src, dst, target):
        copy = pltpu.make_async_remote_copy(
            src_ref=src,
            dst_ref=dst,
            send_sem=self.send.at[self.used],
            recv_sem=self.recv.at[self.used],
            device_id=target,
            device_id_type=MESH,
        )
        self.used += 1
        copy.start()
        self.all[name] = copy

    def arrived(self, name):
        self.all[name].wait_recv()

    def finish(self):
        for copy in self.all.values():
            copy.wait_send()


def step_kernel(
    grad_scale, tokens, cotangent, weight, feedback_in, q_in, input_grad, merged, p_hat_ref, q_next_ref,
    tok, cot, part, hop, side, z_last, z_send, z_first, w_all,
    pa_slots, pb_slots, g1_slots, g2_slots, wide_factor, s_out, s1, s2, s3_out, s3, met,
    feedback, q_ref, send, recv, load_sem, store_sem,
):
    zh, y, x, zl, c = where_am_i()
    mate = device(zh, y, x, zl, 1 - c)
    x_up, x_down = device(zh, y, (x + 1) % 4, zl, c), device(zh, y, (x + 3) % 4, zl, c)
    y_up, y_down = device(zh, (y + 1) % 4, x, zl, c), device(zh, (y + 3) % 4, x, zl, c)
    z_pair, z_across = device(zh, y, x, 1 - zl, c), device(1 - zh, y, x, 1 - zl, c)
    d = lax.axis_index("dp")
    f = lax.axis_index("fsdp")
    plane = x * 4 + y
    column = zh * 4 + zl * 2 + c
    y_of = [device(zh, (y + k) % 4, x, zl, c) for k in range(1, 4)]
    z_of = [device(1 - zh, y, x, zl, c)]
    group_of = [((d + k) % 8, f) for k in range(1, 8)]
    member_of = [(d, (f + k) % 16) for k in range(1, 16)]
    plane_at = [(plane + k) % 16 for k in range(1, 16)]
    plane_of = [device(zh, t % 4, t // 4, zl, c) for t in plane_at]
    column_at = [(column + k) % 8 for k in range(1, 8)]
    column_of = [device(t // 4, y, x, (t // 2) % 2, t % 2) for t in column_at]
    partners = [mate, x_up, x_down, y_up, y_down, z_pair, z_across]

    def first_row(relative, core):
        rx, rz = relative
        return (((x + rx) % 4) * 4 + ((zl + rz) % 2) * 2 + core) * 512

    barrier = pltpu.get_barrier_semaphore()
    for target in partners:
        pl.semaphore_signal(barrier, inc=1, device_id=target, device_id_type=MESH)
    loads = [pltpu.make_async_copy(cotangent, cot.at[0:512], load_sem.at[8])]
    for o, relative in enumerate(ORDER):
        columns = pl.ds(pl.multiple_of(first_row(relative, c), 512), 512)
        loads.append(pltpu.make_async_copy(tokens.at[:, columns], tok.at[o, 0:512], load_sem.at[o]))
    late = [
        pltpu.make_async_copy(feedback_in, feedback, load_sem.at[10]),
        pltpu.make_async_copy(q_in, q_ref, load_sem.at[11]),
    ]
    for load in loads + late:
        load.start()
    pl.semaphore_wait(barrier, len(partners))

    rounds = [[x_up, x_down], [y_up, y_down], [y_up, y_down], [z_pair, z_across], [z_pair, z_across], [mate]]

    def meet(n):
        if n > 0:
            pl.semaphore_wait(met.at[n - 1], len(rounds[n - 1]))
        if n < len(rounds):
            for target in rounds[n]:
                pl.semaphore_signal(met.at[n], inc=1, device_id=target, device_id_type=MESH)

    go = Copies(send, recv)
    go.start(("cot", 1), cotangent.at[:, 512:1024], cot.at[512:1024, 512:1024], mate)
    for o, relative in enumerate(ORDER):
        columns = pl.ds(pl.multiple_of(first_row(relative, 1 - c), 512), 512)
        go.start(("tok", o), tokens.at[:, columns], tok.at[o, 512:1024], mate)
        if o == 0:
            go.start(("cot", 0), cotangent.at[:, 0:512], cot.at[512:1024, 0:512], mate)

    def quarter(of, start=0, size=128):
        return pl.ds(pl.multiple_of(of * 128 + start, 64), size)

    mine = quarter(y)
    below, above = (y + 3) % 4, (y + 1) % 4
    own_shard = pltpu.make_async_copy(weight, w_all.at[SLOT[0, 0]], load_sem.at[9])
    own_shard.start()
    go.start(("wx", 3), weight.at[mine], w_all.at[SLOT[3, 0], mine], x_up)
    go.start(("wx", 1), weight.at[mine], w_all.at[SLOT[1, 0], mine], x_down)
    go.start(("w0", 0), weight.at[0:256], w_all.at[SLOT[0, 1], 0:256], z_across)

    def same(name, relative, rows, target):
        src = w_all.at[SLOT[relative], rows]
        go.start((name, relative), src, src, target)

    def weight_y(relative):
        same("yu", relative, mine, y_up)
        same("yd", relative, mine, y_down)

    def forward_y(relative):
        go.arrived(("yu", relative))
        same("fu", relative, quarter(below, 0, 64), y_up)
        go.arrived(("yd", relative))
        same("fd", relative, quarter(above, 64, 64), y_down)

    def weight_x():
        for rx, start, target in ((3, 0, x_up), (1, 64, x_down)):
            go.arrived(("wx", rx))
            rows = quarter(y, start, 64)
            go.start(("wf", rx), w_all.at[SLOT[rx, 0], rows], w_all.at[SLOT[2, 0], rows], target)
            go.start(("wz", rx), w_all.at[SLOT[rx, 0], mine], w_all.at[SLOT[rx, 1], mine], z_across)
            weight_y((rx, 0))

    def weight_opposite():
        go.arrived(("wf", 3))
        go.arrived(("wf", 1))
        go.start(("wz", 2), w_all.at[SLOT[2, 0], mine], w_all.at[SLOT[2, 1], mine], z_across)
        go.start(("w0", 1), weight.at[256:512], w_all.at[SLOT[0, 1], 256:512], z_across)
        weight_y((2, 0))

    def weight_z(rx):
        go.arrived(("wz", rx))
        weight_y((rx, 1))

    stores = []

    def project(relative):
        n = len(stores)
        slot = SLOT[relative]
        if relative == (0, 0):
            own_shard.wait()
        elif relative == (0, 1):
            go.arrived(("w0", 0))
            go.arrived(("w0", 1))
        else:
            go.arrived(("fu", relative))
            go.arrived(("fd", relative))

        @pl.loop(0, 4)
        def _(i):
            rows = pl.ds(pl.multiple_of(i * 256, 256), 256)
            tok[slot, rows] = lax.dot_general(
                cot[rows], w_all[slot], (((1,), (1,)), ((), ())), preferred_element_type=F32
            ).astype(BF16)

        columns = pl.ds(pl.multiple_of(first_row(relative, c), 512), 512)
        made = tok.at[slot]
        store = pltpu.make_async_copy(made.at[0:512], input_grad.at[:, columns], store_sem.at[n])
        store.start()
        stores.append(store)
        go.start(("out", n), made.at[512:1024], input_grad.at[:, columns], mate)

    def first_partial(color):
        if color == 1:
            loads[0].wait()
            loads[1].wait()
            go.arrived(("tok", 0))
        go.arrived(("cot", color))
        columns = slice(512 * color, 512 * color + 512)

        @pl.loop(0, 2)
        def _(i):
            rows = pl.ds(pl.multiple_of(i * 256, 256), 256)
            part[0, rows, columns] = lax.dot_general(
                tok[0, :, rows], cot[:, columns], (((0,), (0,)), ((), ())), preferred_element_type=F32
            ).astype(BF16)

    def partial(o):
        loads[1 + o].wait()
        go.arrived(("tok", o))

        @pl.loop(0, 2)
        def _(i):
            rows = pl.ds(pl.multiple_of(i * 256, 256), 256)
            part[o, rows] = lax.dot_general(
                tok[o, :, rows], cot[...], (((0,), (0,)), ((), ())), preferred_element_type=F32
            ).astype(BF16)

    START = [0, 0, 512]
    ACROSS = [1, 0, 0]

    def columns_of(s, which):
        return pl.ds(START[s] + 256 * which, 256)

    def opposite(s):
        src = part.at[SLOT[2, ACROSS[s]]]
        go.start(("hop", s, 0), src.at[:, columns_of(s, 0)], hop.at[s, 0], x_up)
        go.start(("hop", s, 1), src.at[:, columns_of(s, 1)], hop.at[s, 1], x_down)

    def beside_up(s):
        src = part.at[SLOT[1, ACROSS[s]]]
        go.start(("side", s, 0, 1), src.at[:, columns_of(s, 1)], side.at[s, 0, :, 256:512], x_up)

    def beside_down(s):
        src = part.at[SLOT[3, ACROSS[s]]]
        go.start(("side", s, 1, 0), src.at[:, columns_of(s, 0)], side.at[s, 1, :, 0:256], x_down)

    def add_into(dst, dst_columns, src, src_columns):
        @pl.loop(0, 4)
        def _(i):
            rows = pl.ds(pl.multiple_of(i * 128, 128), 128)
            dst[rows, dst_columns] = (
                dst[rows, dst_columns].astype(F32) + src[rows, src_columns].astype(F32)
            ).astype(BF16)

    def pass_on(s):
        for which, rx, target in ((0, 1, x_up), (1, 3, x_down)):
            go.arrived(("hop", s, which))
            mine = part.at[SLOT[rx, ACROSS[s]]]
            add_into(mine, columns_of(s, which), hop.at[s, which], pl.ds(0, 256))
            for r in range(PARTS if s == 2 else 1):
                rows = pl.ds(ROWS * r, ROWS) if s == 2 else pl.ds(0, 512)
                go.start(
                    ("side", s, which, which) if s < 2 else ("last", which, r), mine.at[rows, columns_of(s, which)],
                    side.at[s, which, rows, 256 * which : 256 * which + 256], target,
                )

    def sides_arrived(s):
        for which in range(2):
            for columns in range(2):
                go.arrived(("side", s, which, columns))

    def z_exchange(rx):
        go.start(("z1", rx), part.at[SLOT[rx, 1], :, 512:1024], z_first.at[rx], z_pair)

    def z_sum(rx):
        go.arrived(("z1", rx))
        add_into(part.at[SLOT[rx, 0]], pl.ds(512, 512), z_first.at[rx], pl.ds(0, 512))

    def finish_across():
        sides_arrived(0)

        @pl.loop(0, 4)
        def _(i):
            rows = pl.ds(pl.multiple_of(i * 128, 128), 128)
            z_send[rows] = (
                part[SLOT[0, 1], rows, 0:512].astype(F32)
                + side[0, 0, rows].astype(F32)
                + side[0, 1, rows].astype(F32)
            ).astype(BF16)

        for r in range(PARTS):
            rows = pl.ds(ROWS * r, ROWS)
            go.start(("z2", r), z_send.at[rows], z_last.at[rows], z_pair)

    def finish_here(r):
        if r == 0:
            sides_arrived(1)
        go.arrived(("z2", r))

        @pl.loop(r * 4 // PARTS, (r + 1) * 4 // PARTS)
        def _(i):
            rows = pl.ds(pl.multiple_of(i * 128, 128), 128)
            total = (
                part[SLOT[0, 0], rows, 0:512].astype(F32)
                + side[1, 0, rows].astype(F32)
                + side[1, 1, rows].astype(F32)
                + z_last[rows].astype(F32)
            )
            merged[rows, 0:512] = feedback[rows, 0:512] + total * grad_scale

    def finish_second(r):
        if r == 0:
            go.arrived(("side", 2, 0, 1))
            go.arrived(("side", 2, 1, 0))
            go.arrived(("z1", 0))
        for which in range(2):
            go.arrived(("last", which, r))

        @pl.loop(r * 4 // PARTS, (r + 1) * 4 // PARTS)
        def _(i):
            rows = pl.ds(pl.multiple_of(i * 128, 128), 128)
            total = (
                part[SLOT[0, 0], rows, 512:1024].astype(F32)
                + side[2, 0, rows].astype(F32)
                + side[2, 1, rows].astype(F32)
                + z_first[0, rows].astype(F32)
            )
            merged[rows, 512:1024] = feedback[rows, 512:1024] + total * grad_scale

    first_partial(1)
    z_exchange(2)
    first_partial(0)
    opposite(0)
    meet(0)
    partial(1)
    meet(1)
    beside_up(0)
    z_exchange(1)
    weight_x()
    partial(2)
    meet(2)
    beside_down(0)
    z_exchange(3)
    partial(3)
    meet(3)
    z_exchange(0)
    partial(4)
    meet(4)
    opposite(1)
    partial(5)
    meet(5)
    beside_up(1)
    pass_on(0)
    forward_y((3, 0))
    partial(6)
    meet(6)
    beside_down(1)
    z_sum(2)
    opposite(2)
    weight_opposite()
    partial(7)
    forward_y((1, 0))
    weight_z(3)
    weight_z(1)
    for load in late:
        load.wait()
    project((0, 0))
    z_sum(1)
    beside_up(2)
    weight_z(2)
    pass_on(1)
    project((3, 0))
    forward_y((2, 0))
    project((1, 0))
    finish_across()
    z_sum(3)
    beside_down(2)
    forward_y((3, 1))
    project((0, 1))
    forward_y((1, 1))
    pass_on(2)
    forward_y((2, 1))
    project((2, 0))
    project((3, 1))
    for r in range(PARTS):
        finish_here(r)
        finish_second(r)
        rows = slice(ROWS * r, ROWS * r + ROWS)
        p_local = exact(q_ref[...], merged[rows], ((1,), (1,)))
        pa_slots[r, y] = p_local.astype(BF16)
        spread(go, ("pa", r), lambda k: pa_slots.at[r, y], pa_slots.at[r], y, y_of)
    project((1, 1))
    for r in range(PARTS):
        gathered(go, ("pa", r), y_of)
        pb_slots[r, zh] = total_of(pa_slots.at[r], 4).astype(BF16)
        spread(go, ("pb", r), lambda k: pb_slots.at[r, zh], pb_slots.at[r], zh, z_of)
    s_local = None
    for r in range(PARTS):
        gathered(go, ("pb", r), z_of)
        wide_factor[:, ROWS * r : ROWS * r + ROWS] = total_of(pb_slots.at[r], 2) * 0.125
        if r == PARTS - 1:
            slice_of_p = wide_factor[pl.ds(pl.multiple_of(d * 8, 8), 8)]
            g1_slots[f] = exact(slice_of_p, wide_factor[...], ((1,), (1,)))
            spread(go, "g1", lambda k: g1_slots.at[f], g1_slots, f, member_of)
        if (r + 1) * ROWS % 256 == 0:
            rows = slice((r + 1) * ROWS - 256, (r + 1) * ROWS)
            s_part = exact(wide_factor[:, rows], merged[rows], ((1,), (0,)))
            s_local = s_part if s_local is None else s_local + s_part
    factor = wide_factor[...]
    for i in range(4):
        for j in range(4):
            s_out[i * 4 + j] = (s_local[16 * i : 16 * i + 16, 256 * j : 256 * j + 256] * 0.125).astype(BF16)
    spread(go, "s1", lambda k: s_out.at[plane_at[k]], s1, plane, plane_of)
    s1[plane] = s_out[plane]
    project((2, 1))
    gathered(go, "g1", member_of)
    g2_slots[d] = total_of(g1_slots, 16)
    spread(go, "g2", lambda k: g2_slots.at[d], g2_slots, d, group_of)

    gathered(go, "s1", plane_of)
    s2[column] = total_of(s1, 16).astype(BF16)
    spread(go, "s2", lambda k: s2.at[column], s2, column, column_of)
    gathered(go, "g2", group_of)
    group = lax.broadcasted_iota(jnp.int32, (8, 8, 64), 0)
    row = lax.broadcasted_iota(jnp.int32, (8, 8, 64), 1)
    lane = lax.broadcasted_iota(jnp.int32, (8, 8, 64), 2)
    eye = jnp.where(group * 8 + row == lane, 1.0, 0.0).astype(F32)
    work = jnp.concatenate([eye, g2_slots[...]], axis=2)
    row_id = lax.broadcasted_iota(jnp.int32, (8, 8, 128), 0) * 8 + lax.broadcasted_iota(jnp.int32, (8, 8, 128), 1)
    for k in range(0, 24, 4):
        work = eliminate(work, k, row_id)

    gathered(go, "s2", column_of)
    s3_out[...] = total_of(s2, 8).astype(BF16)
    s3[plane] = s3_out[...]
    spread(go, "s3", lambda k: s3_out, s3, plane, plane_of)
    for k in range(24, 64, 4):
        work = eliminate(work, k, row_id)
    lane_id = lax.broadcasted_iota(jnp.int32, (8, 8, 128), 2)
    diagonal = jnp.sum(jnp.where(lane_id == row_id + 64, work, 0.0), axis=2, keepdims=True)
    inverse = (work * (1.0 / jnp.sqrt(diagonal))).reshape(64, 128)[:, :64]
    p_hat_ref[...] = jnp.transpose(exact(inverse, factor, ((1,), (0,))))

    for n in range(8):
        go.arrived(("out", n))
        stores[n].wait()
    gathered(go, "s3", plane_of)
    s_total = jnp.concatenate(
        [jnp.concatenate([s3[i * 4 + j] for j in range(4)], axis=1) for i in range(4)], axis=0
    ).astype(F32)
    q_next_ref[...] = exact(inverse, s_total, ((1,), (0,)))
    go.finish()


def step(tokens, cotangent, weight, feedback, q_t, grad_scale):
    rows, width = feedback.shape
    rank = q_t.shape[0]
    vmem = pl.BlockSpec(memory_space=pltpu.VMEM)
    hbm = pl.BlockSpec(memory_space=pltpu.HBM)
    dma = pltpu.SemaphoreType.DMA
    return pl.pallas_call(
        functools.partial(step_kernel, grad_scale),
        out_shape=(
            pltpu.VMEM(tokens.shape, BF16),
            pltpu.VMEM((rows, width), F32),
            pltpu.VMEM((rows, rank), F32),
            pltpu.VMEM((rank, width), F32),
        ),
        in_specs=[hbm] * 5,
        out_specs=(vmem,) * 4,
        scratch_shapes=[
            pltpu.VMEM((8, 1024, 512), BF16),
            pltpu.VMEM((1024, 1024), BF16),
            pltpu.VMEM((8, 512, 1024), BF16),
            pltpu.VMEM((3, 2, 512, 256), BF16),
            pltpu.VMEM((3, 2, 512, 512), BF16),
            pltpu.VMEM((512, 512), BF16),
            pltpu.VMEM((512, 512), BF16),
            pltpu.VMEM((4, 512, 512), BF16),
            pltpu.VMEM((8, 512, 1024), BF16),
            pltpu.VMEM((PARTS, 4, rank, ROWS), BF16),
            pltpu.VMEM((PARTS, 2, rank, ROWS), BF16),
            pltpu.VMEM((16, 8, rank), F32),
            pltpu.VMEM((8, 8, rank), F32),
            pltpu.VMEM((rank, rows), F32),
            pltpu.VMEM((16, 16, 256), BF16),
            pltpu.VMEM((16, 16, 256), BF16),
            pltpu.VMEM((8, 16, 256), BF16),
            pltpu.VMEM((16, 256), BF16),
            pltpu.VMEM((16, 16, 256), BF16),
            pltpu.SemaphoreType.REGULAR((6,)),
            pltpu.VMEM((rows, width), F32),
            pltpu.VMEM((rank, width), F32),
            dma((N_COPIES,)), dma((N_COPIES,)), dma((12,)), dma((16,)),
        ],
        compiler_params=pltpu.CompilerParams(
            collective_id=2, has_side_effects=True, vmem_limit_bytes=50 * 1024 * 1024
        ),
        name="step",
    )(tokens, cotangent, weight, feedback, q_t)


def results_kernel(made, merged, p_hat, q_next, input_grad, feedback_next, q_out, wide, write_sem):
    writes = [
        pltpu.make_async_copy(made, input_grad, write_sem.at[0]),
        pltpu.make_async_copy(q_next, q_out, write_sem.at[1]),
    ]
    for write in writes:
        write.start()
    half = wide.shape[0] // 2
    for h in range(2):
        rows = pl.ds(h * half, half)
        wide[rows] = merged[rows] - exact(p_hat[rows], q_next[...], ((1,), (0,)))
        writes.append(pltpu.make_async_copy(wide.at[rows], feedback_next.at[rows], write_sem.at[2 + h]))
        writes[2 + h].start()
    for write in writes:
        write.wait()


def results(made, merged, p_hat, q_next):
    vmem = pl.BlockSpec(memory_space=pltpu.VMEM)
    hbm = pl.BlockSpec(memory_space=pltpu.HBM)
    return pl.pallas_call(
        results_kernel,
        out_shape=(
            jax.ShapeDtypeStruct(made.shape, BF16),
            jax.ShapeDtypeStruct(merged.shape, F32),
            jax.ShapeDtypeStruct(q_next.shape, F32),
        ),
        in_specs=[vmem] * 4,
        out_specs=(hbm,) * 3,
        scratch_shapes=[pltpu.VMEM(merged.shape, F32), pltpu.SemaphoreType.DMA((4,))],
        compiler_params=pltpu.CompilerParams(vmem_limit_bytes=16 * 1024 * 1024),
        name="results",
    )(made, merged, p_hat, q_next)


def per_device(tokens, cotangent, weight, feedback, q_factor):
    members = lax.axis_size("fsdp")
    grad_scale = 1.0 / math.sqrt(tokens.shape[0] * members)
    made, merged, p_hat, q_next = step(tokens, cotangent, weight, feedback[0], q_factor.T, grad_scale)
    input_grad, feedback_next, q_next = results(made, merged, p_hat, q_next)
    return (input_grad, q_next.T, feedback_next[None])


def solution(mesh):
    placed = (
        P(("dp", "fsdp"), None),
        P(("dp", "fsdp"), None),
        P("fsdp", None),
        P("dp", "fsdp", None),
        P(),
    )
    return jax.shard_map(
        per_device,
        mesh=mesh,
        in_specs=placed,
        out_specs=(P(("dp", "fsdp"), None), P(), P("dp", "fsdp", None)),
        check_vma=False,
    )
```

```python
import functools
import math

import jax
import jax.numpy as jnp
from jax import lax
from jax.experimental import pallas as pl
from jax.experimental.pallas import tpu as pltpu
from jax.sharding import PartitionSpec as P

MESH = pl.DeviceIdType.MESH
HIGHEST = lax.Precision.HIGHEST
F32 = jnp.float32
BF16 = jnp.bfloat16


def where_am_i():
    d = lax.axis_index("dp")
    f = lax.axis_index("fsdp")
    return d // 4, d % 4, f // 4, (f // 2) % 2, f % 2


def device(zh, y, x, zl, c):
    return (zh * 4 + y, x * 4 + zl * 2 + c)


def exact(left, right, dims):
    return lax.dot_general(left, right, (dims, ((), ())), precision=HIGHEST, preferred_element_type=F32)


def spread(copies, name, src, slots, me, targets):
    for k, target in enumerate(targets):
        copies.start((name, k), src(k), slots.at[me], target)


def gathered(copies, name, targets):
    for k in range(len(targets)):
        copies.arrived((name, k))


def total_of(slots, n):
    total = slots[0].astype(F32)
    for k in range(1, n):
        total = total + slots[k].astype(F32)
    return total


def eliminate(work, k, row_id):
    group, first = k // 8, k % 8
    done, work, row_id = work[:group], work[group:], row_id[group:]
    columns = [jnp.broadcast_to(work[:, :, 64 + k + j : 65 + k + j], work.shape) for j in range(4)]
    rows = [jnp.broadcast_to(work[0, first + j : first + j + 1, :], (8, 128)) for j in range(4)]
    pivot = {}
    for j in range(4):
        for i in range(j, 4):
            pivot[i, j] = jnp.broadcast_to(columns[j][0, first + i : first + i + 1, :], (8, 128))
    for j in range(4):
        inverse = 1.0 / pivot[j, j]
        multiplier = columns[j] * inverse
        for i in range(j + 1, 4):
            columns[i] = columns[i] - multiplier * pivot[i, j]
            scale = pivot[i, j] * inverse
            rows[i] = rows[i] - scale * rows[j]
            for m in range(i, 4):
                pivot[m, i] = pivot[m, i] - scale * pivot[m, j]
        work = work - jnp.where(row_id > k + j, multiplier, 0.0) * rows[j]
    return work if group == 0 else jnp.concatenate([done, work], axis=0)


ORDER = [(2, 1), (1, 1), (3, 1), (0, 1), (2, 0), (1, 0), (3, 0), (0, 0)]
SLOT = {relative: o for o, relative in enumerate(ORDER)}
N_COPIES = 176
PARTS = 4
ROWS = 512 // PARTS


def far_first(n, m, weights):
    def length(step):
        return weights[0] * min(step[0], n - step[0]) + weights[1] * min(step[1], m - step[1])

    return sorted([(i, k) for i in range(n) for k in range(m) if i + k > 0], key=length, reverse=True)


class Copies:
    def __init__(self, send, recv):
        self.send, self.recv, self.used, self.all = send, recv, 0, {}

    def start(self, name, src, dst, target):
        copy = pltpu.make_async_remote_copy(
            src_ref=src,
            dst_ref=dst,
            send_sem=self.send.at[self.used],
            recv_sem=self.recv.at[self.used],
            device_id=target,
            device_id_type=MESH,
        )
        self.used += 1
        copy.start()
        self.all[name] = copy

    def arrived(self, name):
        self.all[name].wait_recv()

    def finish(self):
        for copy in self.all.values():
            copy.wait_send()


def step_kernel(
    grad_scale, tokens, cotangent, weight, feedback_in, q_in, input_grad, merged, p_hat_ref, q_next_ref,
    tok, cot, part, hop, side, z_last, z_send, z_first, w_all,
    pa_slots, pb_slots, g1_slots, g2_slots, wide_factor, s_out, s1, s2, s3_out, s3, met,
    feedback, q_ref, send, recv, load_sem, store_sem,
):
    zh, y, x, zl, c = where_am_i()
    mate = device(zh, y, x, zl, 1 - c)
    x_up, x_down = device(zh, y, (x + 1) % 4, zl, c), device(zh, y, (x + 3) % 4, zl, c)
    y_up, y_down = device(zh, (y + 1) % 4, x, zl, c), device(zh, (y + 3) % 4, x, zl, c)
    z_pair, z_across = device(zh, y, x, 1 - zl, c), device(1 - zh, y, x, 1 - zl, c)
    d = lax.axis_index("dp")
    f = lax.axis_index("fsdp")
    plane = x * 4 + y
    column = zh * 4 + zl * 2 + c
    z = zh * 2 + zl
    y_of = [device(zh, (y + k) % 4, x, zl, c) for k in (2, 1, 3)]
    z_of = [device(1 - zh, y, x, zl, c)]
    group_of = [device((zh + i) % 2, (y + k) % 4, x, zl, c) for i, k in far_first(2, 4, (2, 1))]
    member_of = [
        device(zh, y, (x + i) % 4, (zl + k // 2) % 2, (c + k) % 2) for i, k in far_first(4, 4, (1, 0.4))
    ]
    plane_step = far_first(4, 4, (1, 1))
    plane_at = [((x + i) % 4) * 4 + (y + k) % 4 for i, k in plane_step]
    plane_of = [device(zh, (y + k) % 4, (x + i) % 4, zl, c) for i, k in plane_step]
    column_of = [
        device(((z + i) % 4) // 2, y, x, ((z + i) % 4) % 2, (c + k) % 2) for i, k in far_first(4, 2, (1, 0.1))
    ]
    partners = [mate, x_up, x_down, y_up, y_down, z_pair, z_across]

    def first_row(relative, core):
        rx, rz = relative
        return (((x + rx) % 4) * 4 + ((zl + rz) % 2) * 2 + core) * 512

    barrier = pltpu.get_barrier_semaphore()
    for target in partners:
        pl.semaphore_signal(barrier, inc=1, device_id=target, device_id_type=MESH)
    loads = [pltpu.make_async_copy(cotangent, cot.at[0:512], load_sem.at[8])]
    for o, relative in enumerate(ORDER):
        columns = pl.ds(pl.multiple_of(first_row(relative, c), 512), 512)
        loads.append(pltpu.make_async_copy(tokens.at[:, columns], tok.at[o, 0:512], load_sem.at[o]))
    late = [
        pltpu.make_async_copy(feedback_in, feedback, load_sem.at[10]),
        pltpu.make_async_copy(q_in, q_ref, load_sem.at[11]),
    ]
    for load in loads + late:
        load.start()
    pl.semaphore_wait(barrier, len(partners))

    rounds = [[x_up, x_down], [y_up, y_down], [y_up, y_down], [z_pair, z_across], [z_pair, z_across], [mate]]

    def meet(n):
        if n > 0:
            pl.semaphore_wait(met.at[n - 1], len(rounds[n - 1]))
        if n < len(rounds):
            for target in rounds[n]:
                pl.semaphore_signal(met.at[n], inc=1, device_id=target, device_id_type=MESH)

    go = Copies(send, recv)
    go.start(("cot", 1), cotangent.at[:, 512:1024], cot.at[512:1024, 512:1024], mate)
    for o, relative in enumerate(ORDER):
        columns = pl.ds(pl.multiple_of(first_row(relative, 1 - c), 512), 512)
        go.start(("tok", o), tokens.at[:, columns], tok.at[o, 512:1024], mate)
        if o == 0:
            go.start(("cot", 0), cotangent.at[:, 0:512], cot.at[512:1024, 0:512], mate)

    def quarter(of, start=0, size=128):
        return pl.ds(pl.multiple_of(of * 128 + start, 64), size)

    mine = quarter(y)
    below, above = (y + 3) % 4, (y + 1) % 4
    own_shard = pltpu.make_async_copy(weight, w_all.at[SLOT[0, 0]], load_sem.at[9])
    own_shard.start()
    go.start(("wx", 3), weight.at[mine], w_all.at[SLOT[3, 0], mine], x_up)
    go.start(("wx", 1), weight.at[mine], w_all.at[SLOT[1, 0], mine], x_down)
    go.start(("w0", 0), weight.at[0:256], w_all.at[SLOT[0, 1], 0:256], z_across)

    def same(name, relative, rows, target):
        src = w_all.at[SLOT[relative], rows]
        go.start((name, relative), src, src, target)

    def weight_y(relative):
        same("yu", relative, mine, y_up)
        same("yd", relative, mine, y_down)

    def forward_y(relative):
        go.arrived(("yu", relative))
        same("fu", relative, quarter(below, 0, 64), y_up)
        go.arrived(("yd", relative))
        same("fd", relative, quarter(above, 64, 64), y_down)

    def weight_x():
        for rx, start, target in ((3, 0, x_up), (1, 64, x_down)):
            go.arrived(("wx", rx))
            rows = quarter(y, start, 64)
            go.start(("wf", rx), w_all.at[SLOT[rx, 0], rows], w_all.at[SLOT[2, 0], rows], target)
            go.start(("wz", rx), w_all.at[SLOT[rx, 0], mine], w_all.at[SLOT[rx, 1], mine], z_across)
            weight_y((rx, 0))

    def weight_opposite():
        go.arrived(("wf", 3))
        go.arrived(("wf", 1))
        go.start(("wz", 2), w_all.at[SLOT[2, 0], mine], w_all.at[SLOT[2, 1], mine], z_across)
        go.start(("w0", 1), weight.at[256:512], w_all.at[SLOT[0, 1], 256:512], z_across)
        weight_y((2, 0))

    def weight_z(rx):
        go.arrived(("wz", rx))
        weight_y((rx, 1))

    stores = []

    def project(relative):
        n = len(stores)
        slot = SLOT[relative]
        if relative == (0, 0):
            own_shard.wait()
        elif relative == (0, 1):
            go.arrived(("w0", 0))
            go.arrived(("w0", 1))
        else:
            go.arrived(("fu", relative))
            go.arrived(("fd", relative))

        @pl.loop(0, 4)
        def _(i):
            rows = pl.ds(pl.multiple_of(i * 256, 256), 256)
            tok[slot, rows] = lax.dot_general(
                cot[rows], w_all[slot], (((1,), (1,)), ((), ())), preferred_element_type=F32
            ).astype(BF16)

        columns = pl.ds(pl.multiple_of(first_row(relative, c), 512), 512)
        made = tok.at[slot]
        store = pltpu.make_async_copy(made.at[0:512], input_grad.at[:, columns], store_sem.at[n])
        store.start()
        stores.append(store)
        go.start(("out", n), made.at[512:1024], input_grad.at[:, columns], mate)

    def first_partial(color):
        if color == 1:
            loads[0].wait()
            loads[1].wait()
            go.arrived(("tok", 0))
        go.arrived(("cot", color))
        columns = slice(512 * color, 512 * color + 512)

        @pl.loop(0, 2)
        def _(i):
            rows = pl.ds(pl.multiple_of(i * 256, 256), 256)
            part[0, rows, columns] = lax.dot_general(
                tok[0, :, rows], cot[:, columns], (((0,), (0,)), ((), ())), preferred_element_type=F32
            ).astype(BF16)

    def partial(o):
        loads[1 + o].wait()
        go.arrived(("tok", o))

        @pl.loop(0, 2)
        def _(i):
            rows = pl.ds(pl.multiple_of(i * 256, 256), 256)
            part[o, rows] = lax.dot_general(
                tok[o, :, rows], cot[...], (((0,), (0,)), ((), ())), preferred_element_type=F32
            ).astype(BF16)

    START = [0, 0, 512]
    ACROSS = [1, 0, 0]

    def columns_of(s, which):
        return pl.ds(START[s] + 256 * which, 256)

    def opposite(s):
        src = part.at[SLOT[2, ACROSS[s]]]
        go.start(("hop", s, 0), src.at[:, columns_of(s, 0)], hop.at[s, 0], x_up)
        go.start(("hop", s, 1), src.at[:, columns_of(s, 1)], hop.at[s, 1], x_down)

    def beside_up(s):
        src = part.at[SLOT[1, ACROSS[s]]]
        go.start(("side", s, 0, 1), src.at[:, columns_of(s, 1)], side.at[s, 0, :, 256:512], x_up)

    def beside_down(s):
        src = part.at[SLOT[3, ACROSS[s]]]
        go.start(("side", s, 1, 0), src.at[:, columns_of(s, 0)], side.at[s, 1, :, 0:256], x_down)

    def add_into(dst, dst_columns, src, src_columns):
        @pl.loop(0, 4)
        def _(i):
            rows = pl.ds(pl.multiple_of(i * 128, 128), 128)
            dst[rows, dst_columns] = (
                dst[rows, dst_columns].astype(F32) + src[rows, src_columns].astype(F32)
            ).astype(BF16)

    def pass_on(s):
        for which, rx, target in ((0, 1, x_up), (1, 3, x_down)):
            go.arrived(("hop", s, which))
            mine = part.at[SLOT[rx, ACROSS[s]]]
            add_into(mine, columns_of(s, which), hop.at[s, which], pl.ds(0, 256))
            for r in range(PARTS if s == 2 else 1):
                rows = pl.ds(ROWS * r, ROWS) if s == 2 else pl.ds(0, 512)
                go.start(
                    ("side", s, which, which) if s < 2 else ("last", which, r), mine.at[rows, columns_of(s, which)],
                    side.at[s, which, rows, 256 * which : 256 * which + 256], target,
                )

    def sides_arrived(s):
        for which in range(2):
            for columns in range(2):
                go.arrived(("side", s, which, columns))

    def z_exchange(rx):
        go.start(("z1", rx), part.at[SLOT[rx, 1], :, 512:1024], z_first.at[rx], z_pair)

    def z_sum(rx):
        go.arrived(("z1", rx))
        add_into(part.at[SLOT[rx, 0]], pl.ds(512, 512), z_first.at[rx], pl.ds(0, 512))

    def finish_across():
        sides_arrived(0)

        @pl.loop(0, 4)
        def _(i):
            rows = pl.ds(pl.multiple_of(i * 128, 128), 128)
            z_send[rows] = (
                part[SLOT[0, 1], rows, 0:512].astype(F32)
                + side[0, 0, rows].astype(F32)
                + side[0, 1, rows].astype(F32)
            ).astype(BF16)

        for r in range(PARTS):
            rows = pl.ds(ROWS * r, ROWS)
            go.start(("z2", r), z_send.at[rows], z_last.at[rows], z_pair)

    def finish_here(r):
        if r == 0:
            sides_arrived(1)
        go.arrived(("z2", r))

        @pl.loop(r * 4 // PARTS, (r + 1) * 4 // PARTS)
        def _(i):
            rows = pl.ds(pl.multiple_of(i * 128, 128), 128)
            total = (
                part[SLOT[0, 0], rows, 0:512].astype(F32)
                + side[1, 0, rows].astype(F32)
                + side[1, 1, rows].astype(F32)
                + z_last[rows].astype(F32)
            )
            merged[rows, 0:512] = feedback[rows, 0:512] + total * grad_scale

    def finish_second(r):
        if r == 0:
            go.arrived(("side", 2, 0, 1))
            go.arrived(("side", 2, 1, 0))
            go.arrived(("z1", 0))
        for which in range(2):
            go.arrived(("last", which, r))

        @pl.loop(r * 4 // PARTS, (r + 1) * 4 // PARTS)
        def _(i):
            rows = pl.ds(pl.multiple_of(i * 128, 128), 128)
            total = (
                part[SLOT[0, 0], rows, 512:1024].astype(F32)
                + side[2, 0, rows].astype(F32)
                + side[2, 1, rows].astype(F32)
                + z_first[0, rows].astype(F32)
            )
            merged[rows, 512:1024] = feedback[rows, 512:1024] + total * grad_scale

    first_partial(1)
    z_exchange(2)
    first_partial(0)
    opposite(0)
    meet(0)
    partial(1)
    meet(1)
    beside_up(0)
    z_exchange(1)
    weight_x()
    partial(2)
    meet(2)
    beside_down(0)
    z_exchange(3)
    partial(3)
    meet(3)
    z_exchange(0)
    partial(4)
    meet(4)
    opposite(1)
    partial(5)
    meet(5)
    beside_up(1)
    pass_on(0)
    forward_y((3, 0))
    partial(6)
    meet(6)
    beside_down(1)
    z_sum(2)
    opposite(2)
    weight_opposite()
    partial(7)
    forward_y((1, 0))
    weight_z(3)
    weight_z(1)
    for load in late:
        load.wait()
    project((0, 0))
    z_sum(1)
    beside_up(2)
    weight_z(2)
    pass_on(1)
    project((3, 0))
    forward_y((2, 0))
    project((1, 0))
    finish_across()
    z_sum(3)
    beside_down(2)
    forward_y((3, 1))
    project((0, 1))
    forward_y((1, 1))
    pass_on(2)
    forward_y((2, 1))
    project((2, 0))
    project((3, 1))
    for r in range(PARTS):
        finish_here(r)
        finish_second(r)
        rows = slice(ROWS * r, ROWS * r + ROWS)
        p_local = exact(q_ref[...], merged[rows], ((1,), (1,)))
        pa_slots[r, y] = p_local.astype(BF16)
        spread(go, ("pa", r), lambda k: pa_slots.at[r, y], pa_slots.at[r], y, y_of)
    project((1, 1))
    for r in range(PARTS):
        gathered(go, ("pa", r), y_of)
        pb_slots[r, zh] = total_of(pa_slots.at[r], 4).astype(BF16)
        spread(go, ("pb", r), lambda k: pb_slots.at[r, zh], pb_slots.at[r], zh, z_of)
    s_local = None
    for r in range(PARTS):
        gathered(go, ("pb", r), z_of)
        wide_factor[:, ROWS * r : ROWS * r + ROWS] = total_of(pb_slots.at[r], 2) * 0.125
        if r == PARTS - 1:
            slice_of_p = wide_factor[pl.ds(pl.multiple_of(d * 8, 8), 8)]
            g1_slots[f] = exact(slice_of_p, wide_factor[...], ((1,), (1,)))
            spread(go, "g1", lambda k: g1_slots.at[f], g1_slots, f, member_of)
        if (r + 1) * ROWS % 256 == 0:
            rows = slice((r + 1) * ROWS - 256, (r + 1) * ROWS)
            s_part = exact(wide_factor[:, rows], merged[rows], ((1,), (0,)))
            s_local = s_part if s_local is None else s_local + s_part
    factor = wide_factor[...]
    for i in range(4):
        for j in range(4):
            s_out[i * 4 + j] = (s_local[16 * i : 16 * i + 16, 256 * j : 256 * j + 256] * 0.125).astype(BF16)
    spread(go, "s1", lambda k: s_out.at[plane_at[k]], s1, plane, plane_of)
    s1[plane] = s_out[plane]
    project((2, 1))
    gathered(go, "g1", member_of)
    g2_slots[d] = total_of(g1_slots, 16)
    spread(go, "g2", lambda k: g2_slots.at[d], g2_slots, d, group_of)

    gathered(go, "s1", plane_of)
    s2[column] = total_of(s1, 16).astype(BF16)
    spread(go, "s2", lambda k: s2.at[column], s2, column, column_of)
    gathered(go, "g2", group_of)
    group = lax.broadcasted_iota(jnp.int32, (8, 8, 64), 0)
    row = lax.broadcasted_iota(jnp.int32, (8, 8, 64), 1)
    lane = lax.broadcasted_iota(jnp.int32, (8, 8, 64), 2)
    eye = jnp.where(group * 8 + row == lane, 1.0, 0.0).astype(F32)
    work = jnp.concatenate([eye, g2_slots[...]], axis=2)
    row_id = lax.broadcasted_iota(jnp.int32, (8, 8, 128), 0) * 8 + lax.broadcasted_iota(jnp.int32, (8, 8, 128), 1)
    for k in range(0, 24, 4):
        work = eliminate(work, k, row_id)

    gathered(go, "s2", column_of)
    s3_out[...] = total_of(s2, 8).astype(BF16)
    s3[plane] = s3_out[...]
    spread(go, "s3", lambda k: s3_out, s3, plane, plane_of)
    for k in range(24, 64, 4):
        work = eliminate(work, k, row_id)
    lane_id = lax.broadcasted_iota(jnp.int32, (8, 8, 128), 2)
    diagonal = jnp.sum(jnp.where(lane_id == row_id + 64, work, 0.0), axis=2, keepdims=True)
    inverse = (work * (1.0 / jnp.sqrt(diagonal))).reshape(64, 128)[:, :64]
    p_hat_ref[...] = jnp.transpose(exact(inverse, factor, ((1,), (0,))))

    for n in range(8):
        go.arrived(("out", n))
        stores[n].wait()
    gathered(go, "s3", plane_of)
    s_total = jnp.concatenate(
        [jnp.concatenate([s3[i * 4 + j] for j in range(4)], axis=1) for i in range(4)], axis=0
    ).astype(F32)
    q_next_ref[...] = exact(inverse, s_total, ((1,), (0,)))
    go.finish()


def step(tokens, cotangent, weight, feedback, q_t, grad_scale):
    rows, width = feedback.shape
    rank = q_t.shape[0]
    vmem = pl.BlockSpec(memory_space=pltpu.VMEM)
    hbm = pl.BlockSpec(memory_space=pltpu.HBM)
    dma = pltpu.SemaphoreType.DMA
    return pl.pallas_call(
        functools.partial(step_kernel, grad_scale),
        out_shape=(
            pltpu.VMEM(tokens.shape, BF16),
            pltpu.VMEM((rows, width), F32),
            pltpu.VMEM((rows, rank), F32),
            pltpu.VMEM((rank, width), F32),
        ),
        in_specs=[hbm] * 5,
        out_specs=(vmem,) * 4,
        scratch_shapes=[
            pltpu.VMEM((8, 1024, 512), BF16),
            pltpu.VMEM((1024, 1024), BF16),
            pltpu.VMEM((8, 512, 1024), BF16),
            pltpu.VMEM((3, 2, 512, 256), BF16),
            pltpu.VMEM((3, 2, 512, 512), BF16),
            pltpu.VMEM((512, 512), BF16),
            pltpu.VMEM((512, 512), BF16),
            pltpu.VMEM((4, 512, 512), BF16),
            pltpu.VMEM((8, 512, 1024), BF16),
            pltpu.VMEM((PARTS, 4, rank, ROWS), BF16),
            pltpu.VMEM((PARTS, 2, rank, ROWS), BF16),
            pltpu.VMEM((16, 8, rank), F32),
            pltpu.VMEM((8, 8, rank), F32),
            pltpu.VMEM((rank, rows), F32),
            pltpu.VMEM((16, 16, 256), BF16),
            pltpu.VMEM((16, 16, 256), BF16),
            pltpu.VMEM((8, 16, 256), BF16),
            pltpu.VMEM((16, 256), BF16),
            pltpu.VMEM((16, 16, 256), BF16),
            pltpu.SemaphoreType.REGULAR((6,)),
            pltpu.VMEM((rows, width), F32),
            pltpu.VMEM((rank, width), F32),
            dma((N_COPIES,)), dma((N_COPIES,)), dma((12,)), dma((16,)),
        ],
        compiler_params=pltpu.CompilerParams(
            collective_id=2, has_side_effects=True, vmem_limit_bytes=50 * 1024 * 1024
        ),
        name="step",
    )(tokens, cotangent, weight, feedback, q_t)


def results_kernel(made, merged, p_hat, q_next, input_grad, feedback_next, q_out, wide, write_sem):
    writes = [
        pltpu.make_async_copy(made, input_grad, write_sem.at[0]),
        pltpu.make_async_copy(q_next, q_out, write_sem.at[1]),
    ]
    for write in writes:
        write.start()
    half = wide.shape[0] // 2
    for h in range(2):
        rows = pl.ds(h * half, half)
        wide[rows] = merged[rows] - exact(p_hat[rows], q_next[...], ((1,), (0,)))
        writes.append(pltpu.make_async_copy(wide.at[rows], feedback_next.at[rows], write_sem.at[2 + h]))
        writes[2 + h].start()
    for write in writes:
        write.wait()


def results(made, merged, p_hat, q_next):
    vmem = pl.BlockSpec(memory_space=pltpu.VMEM)
    hbm = pl.BlockSpec(memory_space=pltpu.HBM)
    return pl.pallas_call(
        results_kernel,
        out_shape=(
            jax.ShapeDtypeStruct(made.shape, BF16),
            jax.ShapeDtypeStruct(merged.shape, F32),
            jax.ShapeDtypeStruct(q_next.shape, F32),
        ),
        in_specs=[vmem] * 4,
        out_specs=(hbm,) * 3,
        scratch_shapes=[pltpu.VMEM(merged.shape, F32), pltpu.SemaphoreType.DMA((4,))],
        compiler_params=pltpu.CompilerParams(vmem_limit_bytes=16 * 1024 * 1024),
        name="results",
    )(made, merged, p_hat, q_next)


def per_device(tokens, cotangent, weight, feedback, q_factor):
    members = lax.axis_size("fsdp")
    grad_scale = 1.0 / math.sqrt(tokens.shape[0] * members)
    made, merged, p_hat, q_next = step(tokens, cotangent, weight, feedback[0], q_factor.T, grad_scale)
    input_grad, feedback_next, q_next = results(made, merged, p_hat, q_next)
    return (input_grad, q_next.T, feedback_next[None])


def solution(mesh):
    placed = (
        P(("dp", "fsdp"), None),
        P(("dp", "fsdp"), None),
        P("fsdp", None),
        P("dp", "fsdp", None),
        P(),
    )
    return jax.shard_map(
        per_device,
        mesh=mesh,
        in_specs=placed,
        out_specs=(P(("dp", "fsdp"), None), P(), P("dp", "fsdp", None)),
        check_vma=False,
    )
```
